128 devices in a mesh: row: 16 (over y, z), col: 8 (over x, core).
Axes of the slice: x: 4, y: 4, z: 4, core: 2. Of those that a mesh axis runs over, the one named last changes fastest.
Arguments:
- points: bfloat16 [64, 262144], P(None, ('row', 'col')), may hold values from -6 to 6
- weights: float32 [16, 262144], P(None, ('row', 'col')), may hold values from -1.2 to 1.2
- targets: float32 [16, 262144], P(None, ('row', 'col')), may hold values from -6 to 6
- block_index: int32 [1, 16384], replicated, may hold values from 0 to 262143, as said below
Outputs:
- weights_out: float32 [16, 262144], P(None, ('row', 'col'))
- residual: float32 [16, 16384], P(None, ('row', 'col'))
The draws below stay inside these ranges and needn't reach their ends.
Inputs may be any that keep to these rules, and one draw needn't show every extreme that they name: `block_index`: each row is increasing. Point p is held by the device of flat index p // 2048 (row index first). Each aligned run of 2048 points holds at most 256 entries of a row, and some run exactly 256; each aligned run of 16384 points holds exactly 1024 entries of a row.
All inputs are finite; a program needn't handle non-finite values.
Results may differ from the reference program's by a relative error of at most 0.028.
Values may be sent and summed in bfloat16 or wider, within the bound.
A program may use at most 64 MiB of HBM per device.

```python
import jax
import jax.numpy as jnp
from jax import lax

F = 64
TGT = 16
RANK = 256
BLK = 16384
STEPS = 1
CG_ITERS = 2
PTS_DEV = 2048
NPTS = 262144
GROUP_PTS = 16384


def draw_block_index(key, part):
    devices = NPTS // PTS_DEV
    columns = GROUP_PTS // PTS_DEV
    groups = devices // columns
    mean_load = BLK // devices
    stacked = []
    for outer in range(STEPS):
        keys = jax.random.split(jax.random.fold_in(key, 101 + outer), 4)
        spread = jax.random.randint(keys[0], (groups, columns // 2), 0, mean_load + 1)
        target_group = jax.random.randint(keys[1], (), 0, groups)
        is_target = (jnp.arange(groups, dtype=jnp.int32) == target_group)[:, None]
        spread = jnp.where(is_target, mean_load, spread)
        counts = jnp.concatenate([mean_load - spread, mean_load + spread], axis=1)
        scores = jax.random.randint(keys[2], (groups, columns), 0, 1 << 20) * columns + jnp.arange(columns)[None, :]
        ordering = jnp.argsort(scores, axis=1)
        ordering = jnp.where(is_target, jnp.arange(columns, dtype=ordering.dtype)[None, :], ordering)
        counts = jnp.take_along_axis(counts, ordering, axis=1).reshape(devices)
        tickets = jax.random.randint(keys[3], (devices, PTS_DEV), 0, 1 << 16) * PTS_DEV + jnp.arange(PTS_DEV)[None, :]
        standing = jnp.argsort(jnp.argsort(tickets, axis=1), axis=1)
        selected = (standing < counts[:, None]).reshape(devices * PTS_DEV)
        positions = jnp.nonzero(selected, size=BLK)[0].astype(jnp.int32)
        stacked.append(positions)
    return jnp.stack(stacked)


def steps_of(rng, dims, shards, least, top_value):
    factor_of, own = 1.0, jax.random.fold_in(rng, 6)
    for position, shards_of in shards:
        draws = jnp.exp(jax.random.uniform(jax.random.fold_in(own, position), (shards_of,), jnp.float32, least / len(shards), top_value / len(shards)))
        factor_of = factor_of * jnp.repeat(draws, dims[position] // shards_of).reshape([-1 if axis == position else 1 for axis in range(len(dims))])
    return factor_of


def normal_values(own_key, dims, deviation, limit, cuts=(), kind=jnp.bfloat16):
    values = jax.random.normal(own_key, dims, jnp.float32) * deviation
    if len(cuts) > 0:
        values = steps_of(own_key, dims, cuts, -0.22, 0.18) * values
    return jnp.clip(values, min=-limit, max=limit).astype(kind)


def setup_inputs(seed: int = 0) -> dict:
    streams_of = jax.random.split(jax.random.key(seed), 5)
    points = normal_values(streams_of[0], (F, NPTS), 1.0, 6.0, ((1, 128),))
    weights = normal_values(streams_of[1], (TGT, NPTS), 0.2, 1.2, ((1, 128),), jnp.float32)
    targets = normal_values(streams_of[2], (TGT, NPTS), 1.0, 6.0, ((1, 128),), jnp.float32)
    block_index = draw_block_index(jax.random.fold_in(streams_of[4], 71), 0)
    return dict(points=points, weights=weights, targets=targets, block_index=block_index)


ridge = 1.0

def point_squares(points):
    values = points.astype(jnp.float32)
    return jnp.sum(values * values, axis=0)

def kernel_block(left, right, left_sq, right_sq):
    cross = lax.dot_general(left.astype(jnp.float32), right.astype(jnp.float32), (((0,), (0,)), ((), ())), preferred_element_type=jnp.float32)
    return jnp.exp(-(2.0 / left.shape[0]) * (left_sq[:, None] + right_sq[None, :] - 2.0 * cross))

def solve_inner(chol, projected):
    middle = lax.linalg.triangular_solve(chol, projected.T, left_side=True, lower=True)
    return lax.linalg.triangular_solve(chol, middle, left_side=True, lower=True, transpose_a=True).T

def reference(points, weights, targets, block_index):
    squares_all = point_squares(points)
    stretches = NPTS // PTS_DEV
    span = min(BLK, 2048)
    residual = jnp.zeros((TGT, BLK), jnp.float32)
    for step in range(STEPS):
        chosen = block_index[step]
        block_pts = points[:, chosen]
        block_sq = squares_all[chosen]
        weights_bf = weights.astype(jnp.bfloat16)

        def add_stretch(index, total):
            begin = index * PTS_DEV
            some_pts = lax.dynamic_slice_in_dim(points, begin, PTS_DEV, 1)
            some_sq = lax.dynamic_slice_in_dim(squares_all, begin, PTS_DEV, 0)
            some_w = lax.dynamic_slice_in_dim(weights_bf, begin, PTS_DEV, 1)
            kern = kernel_block(some_pts, block_pts, some_sq, block_sq).astype(jnp.bfloat16)
            return total + jnp.dot(some_w.astype(jnp.float32), kern.astype(jnp.float32), preferred_element_type=jnp.float32)
        slab = lax.fori_loop(0, stretches, add_stretch, jnp.zeros((TGT, BLK), jnp.float32))
        rhs = targets[:, chosen] - ridge * weights[:, chosen] - slab
        marks_pts = block_pts[:, :RANK]
        marks_sq = block_sq[:RANK]
        sketch = kernel_block(block_pts, marks_pts, block_sq, marks_sq)
        gram = jnp.dot(sketch.T, sketch, precision=lax.Precision.HIGHEST)
        inner = ridge * kernel_block(marks_pts, marks_pts, marks_sq, marks_sq) + gram
        chol = jnp.linalg.cholesky(inner)

        def precondition(vector):
            projected = jnp.dot(vector, sketch, precision=lax.Precision.HIGHEST)
            solved = solve_inner(chol, projected)
            return (vector - jnp.dot(solved, sketch.T, precision=lax.Precision.HIGHEST)) / ridge

        def apply_block(direction):
            direction_bf = direction.astype(jnp.bfloat16)

            def add_rows(index, total):
                left = lax.dynamic_slice_in_dim(block_pts, index * span, span, 1)
                left_sq = lax.dynamic_slice_in_dim(block_sq, index * span, span, 0)
                kern = kernel_block(left, block_pts, left_sq, block_sq).astype(jnp.bfloat16)
                part = lax.dot_general(direction_bf.astype(jnp.float32), kern.astype(jnp.float32), (((1,), (1,)), ((), ())), preferred_element_type=jnp.float32)
                return lax.dynamic_update_slice_in_dim(total, part, index * span, 1)
            image = lax.fori_loop(0, BLK // span, add_rows, jnp.zeros((TGT, BLK), jnp.float32))
            return image + ridge * direction
        residual = rhs
        delta = jnp.zeros((TGT, BLK), jnp.float32)
        precond = precondition(residual)
        direction = precond
        inner_rz = jnp.sum(residual * precond, axis=1)
        for turn in range(CG_ITERS):
            image = apply_block(direction)
            alpha = inner_rz / jnp.sum(direction * image, axis=1)
            delta = delta + alpha[:, None] * direction
            residual = residual - alpha[:, None] * image
            if turn + 1 < CG_ITERS:
                precond = precondition(residual)
                fresh = jnp.sum(residual * precond, axis=1)
                direction = precond + (fresh / inner_rz)[:, None] * direction
                inner_rz = fresh
        weights = weights.at[:, chosen].add(delta)
    return (weights, residual)
```

```python
import math

import jax
import jax.numpy as jnp
from jax import lax
from jax.experimental import pallas as pl
from jax.experimental.pallas import tpu as pltpu
from jax.sharding import Mesh
from jax.sharding import PartitionSpec as P

RANK = 256
ridge = 1.0
AXES = ("row_0", "row_1", "col_0", "col_1")
MESH = pl.DeviceIdType.MESH
HI = lax.Precision.HIGHEST
F32 = jnp.float32
BF16 = jnp.bfloat16
LOG2E = math.log2(math.e)
TAIL = 16


def wrap(value, size):
    return lax.rem(value, size)


class Place:
    def __init__(self):
        self.sizes = tuple(lax.axis_size(a) for a in AXES)
        self.at = tuple(lax.axis_index(a) for a in AXES)
        ny, nz, nx, nc = self.sizes
        self.rows, self.cols = ny * nz, nx * nc
        self.row = self.at[0] * nz + self.at[1]
        self.col = self.at[2] * nc + self.at[3]
        self.device = self.row * self.cols + self.col

        def hops(step, size):
            return min(step, size - step)

        self.row_steps = sorted(
            ((a, b) for a in range(ny) for b in range(nz) if a or b),
            key=lambda s: -(hops(s[0], ny) + hops(s[1], nz)),
        )
        self.col_steps = sorted(
            ((a, b) for a in range(nx) for b in range(nc) if a or b),
            key=lambda s: -(2 * hops(s[0], nx) + s[1]),
        )

    def row_peer(self, step):
        y = wrap(self.at[0] + step[0], self.sizes[0])
        z = wrap(self.at[1] + step[1], self.sizes[1])
        return y * self.sizes[1] + z, (y, z, self.at[2], self.at[3])

    def col_peer(self, step):
        x = wrap(self.at[2] + step[0], self.sizes[2])
        c = wrap(self.at[3] + step[1], self.sizes[3])
        return x * self.sizes[3] + c, (self.at[0], self.at[1], x, c)

    def x_peers(self):
        out = []
        for step in range(1, self.sizes[2]):
            x = wrap(self.at[2] + step, self.sizes[2])
            out.append((x, (self.at[0], self.at[1], x, self.at[3])))
        return out

    def twin(self):
        return self.col_peer((0, 1))[1]

    def row_peers(self):
        return [self.row_peer(s) for s in self.row_steps]

    def col_peers(self):
        return [self.col_peer(s) for s in self.col_steps]

    def row_before(self, k):
        ny, nz = self.sizes[:2]
        steps = sorted(
            ((a, b) for a in range(ny) for b in range(nz) if a or b),
            key=lambda s: (min(s[0], ny - s[0]) + min(s[1], nz - s[1]), s),
        )
        ys = sum(a << (2 * i) for i, (a, _) in enumerate(steps))
        zs = sum(b << (2 * i) for i, (_, b) in enumerate(steps))
        ys, zs = (lax.rem(jnp.right_shift(jnp.int32(v), 2 * (k - 1)), 4) for v in (ys, zs))
        behind = (wrap(self.at[0] + ny - ys, ny), wrap(self.at[1] + nz - zs, nz))
        ahead = (wrap(self.at[0] + ys, ny), wrap(self.at[1] + zs, nz))
        return behind[0] * nz + behind[1], behind + self.at[2:], ahead + self.at[2:]

    def greet(self):
        barrier = pltpu.get_barrier_semaphore()
        for _, peer in self.row_peers() + self.col_peers():
            pl.semaphore_signal(barrier, inc=1, device_id=peer, device_id_type=MESH)

    def enter(self):
        pl.semaphore_wait(pltpu.get_barrier_semaphore(), self.rows + self.cols - 2)


class Links:
    def __init__(self, sends, recvs):
        self.sends, self.recvs, self.used, self.copies = sends, recvs, 0, []

    def start(self, peers, source, target):
        started = []
        for index, peer in peers:
            copy = pltpu.make_async_remote_copy(
                src_ref=source(index),
                dst_ref=target,
                send_sem=self.sends.at[self.used],
                recv_sem=self.recvs.at[self.used],
                device_id=peer,
                device_id_type=MESH,
            )
            copy.start()
            self.used += 1
            started.append(copy)
        self.copies += started
        return started

    def drain(self):
        for copy in self.copies:
            copy.wait_send()


def arrive(copies):
    for copy in copies:
        copy.wait_recv()


def lanes(index, width):
    return pl.ds(pl.multiple_of(index * width, width), width)


def thirds(value):
    high = value.astype(BF16).astype(F32)
    rest = value - high
    middle = rest.astype(BF16).astype(F32)
    return high, middle, (rest - middle).astype(BF16).astype(F32)


def tail_rows(values, first):
    squares = -0.5 * jnp.sum(values * values, axis=0, keepdims=True)
    parts = thirds(squares)
    shape = (TAIL, values.shape[1])
    at = lax.broadcasted_iota(jnp.int32, shape, 0)
    ones = 8 - first
    rows = jnp.where((at >= ones) & (at < ones + 3), 1.0, 0.0)
    for i in range(3):
        rows = jnp.where(at == first + i, jnp.broadcast_to(parts[i], shape), rows)
    return rows


def as_left(block):
    values = block.astype(F32)
    body = values.shape[0] - TAIL
    left = jnp.concatenate([values[:body], values[body + 8 :], values[body : body + 8]], axis=0)
    return left.T


def kernel_of(left, right, scale):
    return jnp.exp2(scale * jnp.dot(left, right, preferred_element_type=F32))


def total(ref):
    value = ref[0].astype(F32)
    for i in range(1, ref.shape[0]):
        value = value + ref[i].astype(F32)
    return value


def inverse_8(rows, lane):
    shape = (8, 128)
    sub = lax.broadcasted_iota(jnp.int32, shape, 0)
    cols = [jnp.broadcast_to(rows[:, lane + j : lane + j + 1], shape) for j in range(8)]
    for k in range(8):
        pivot = 1.0 / jnp.broadcast_to(cols[k][k : k + 1, :], shape)
        here = sub == k
        column = cols[k]
        for j in range(8):
            if j != k:
                factor = jnp.broadcast_to(cols[j][k : k + 1, :], shape) * pivot
                cols[j] = jnp.where(here, factor, cols[j] - column * factor)
        cols[k] = jnp.where(here, pivot, -column * pivot)
    return cols


def sweep_8(rows, b):
    shape = (8, 128)
    rows = list(rows)
    lane = lax.broadcasted_iota(jnp.int32, shape, 1)
    sub = lax.broadcasted_iota(jnp.int32, shape, 0)
    cols = inverse_8(rows[b], 8 * b)
    inside = (lane >= 8 * b) & (lane < 8 * b + 8)
    right = jnp.where(inside, (lane - 8 * b == sub).astype(F32), rows[b])
    new = None
    for j in range(8):
        term = cols[j] * jnp.broadcast_to(right[j : j + 1, :], shape)
        new = term if new is None else new + term
    spread = [jnp.broadcast_to(new[j : j + 1, :], shape) for j in range(8)]
    for i in range(4):
        if i != b:
            acc = None
            for j in range(8):
                at = 8 * b + j
                term = jnp.broadcast_to(rows[i][:, at : at + 1], shape) * spread[j]
                acc = term if acc is None else acc + term
            rows[i] = jnp.where(inside, 0.0, rows[i]) - acc
    rows[b] = new
    return rows


class Sweep:
    def __init__(self, matrix, k):
        self.matrix, self.at = matrix, pl.multiple_of(k * 32, 32)
        size = matrix.shape[0]
        self.rows = matrix[pl.ds(self.at, 32), :]
        block = pltpu.roll(self.rows, lax.rem(size - self.at, size), 1)[:, :128]
        self.small = [block[8 * i : 8 * i + 8, :] for i in range(4)]

    def inner(self, b):
        self.small = sweep_8(self.small, b)

    def finish(self):
        matrix, at, size = self.matrix, self.at, self.matrix.shape[0]
        lane = lax.broadcasted_iota(jnp.int32, (32, size), 1)
        sub = lax.broadcasted_iota(jnp.int32, (32, size), 0)
        wide = lax.broadcasted_iota(jnp.int32, (size, size), 1)
        inv = jnp.concatenate(self.small, axis=0)[:, :32]
        inside = (lane >= at) & (lane < at + 32)
        right = jnp.where(inside, (lane - at == sub).astype(F32), self.rows)
        new = jnp.dot(inv, right, precision=HI, preferred_element_type=F32)
        left = jnp.where(lane < at, -self.rows, self.rows)
        update = lax.dot_general(
            left, new, (((0,), (0,)), ((), ())), precision=HI, preferred_element_type=F32
        )
        matrix[...] = jnp.where((wide >= at) & (wide < at + 32), 0.0, matrix[...]) - update
        matrix[pl.ds(at, 32), :] = new


def step_kernel(points_in, weights_in, targets_in, index_in, weights_out, residual, *scratch):
    (
        points, weights, targets, index,
        piece, vpiece, pin, vin, share, block, marks,
        own_left, col_left, weights_bf, sketch,
        gram_part, gram_in, gram_own, gram_all, inner, inverse,
        part_mine, part_other, part_twin, part_sum, part_in, cut_part, cut_in, tile,
        half_sketch, proj_own, proj_in, proj_sum, proj_row, proj_all, proj_out,
        dots_own, dots_row, dots_sum, dots_col,
        dir_own, dir_all, dir_f32, dir_col, im_part, im_in, moved,
        sends, recvs, loads, mark_s, mark_r, ag_s, ag_r, fw_s, fw_r, rs_s, rs_r, tw_s, tw_r,
    ) = scratch
    me = Place()
    rows, _, group = block.shape
    here = index_in.at[:, lanes(me.row, group)]
    pairs = [(points_in, points), (here, index), (targets_in, targets), (weights_in, weights)]
    taken = [pltpu.make_async_copy(a, b, loads.at[i]) for i, (a, b) in enumerate(pairs)]
    for copy in taken:
        copy.start()
    me.greet()
    links = Links(sends, recvs)
    for copy in taken:
        copy.wait()
    features, owned = points.shape
    count = weights.shape[0]
    width = group // me.cols
    half = group // 2
    span = min(512, owned)
    scale = 4.0 / features * LOG2E
    pieces = [slice(c * span, (c + 1) * span) for c in range(owned // span)]
    my_lanes = lanes(me.col, width)

    local = index[...] - me.device * owned
    own = targets[...] - ridge * weights[...]
    own = [p.astype(BF16) for p in thirds(own)]
    acc = None
    for c, cut in enumerate(pieces):
        at = lax.broadcasted_iota(jnp.int32, (span, group), 0) + c * span
        chosen = jnp.where(at == local, 1.0, 0.0).astype(BF16)
        left = jnp.concatenate([points[:, cut]] + [p[:, cut] for p in own], axis=0)
        some = jnp.dot(left, chosen, preferred_element_type=F32)
        acc = some if acc is None else acc + some
    for c in range(me.cols):
        cut = slice(c * width, (c + 1) * width)
        piece[c] = acc[:features, cut].astype(BF16)
        parts = acc[features:, cut]
        vpiece[c] = parts[:count] + (parts[count : 2 * count] + parts[2 * count :])
    me.enter()
    first = links.start(me.col_peers(), lambda c: piece.at[c], pin.at[me.col])
    pin[me.col] = piece[me.col]
    vin[me.col] = vpiece[me.col]
    for cut in pieces:
        some = points[:, cut].astype(F32)
        left = jnp.concatenate([some, tail_rows(some, 8)], axis=0)
        own_left[cut, :] = left.T.astype(BF16)
    weights_bf[...] = weights[...].astype(BF16)
    arrive(first)
    mine = total(pin)
    mine = jnp.concatenate([mine, tail_rows(mine, 0)], axis=0).astype(BF16)
    share[...] = mine
    block[me.row, :, my_lanes] = mine
    first = links.start(me.col_peers(), lambda c: share, block.at[me.row, :, my_lanes])
    second = links.start(me.col_peers(), lambda c: vpiece.at[c], vin.at[me.col])
    arrive(first)

    def mark_copy(i):
        return pltpu.make_async_remote_copy(
            src_ref=block.at[0, :, pl.ds(0, RANK)],
            dst_ref=marks,
            send_sem=mark_s.at[i],
            recv_sem=mark_r,
            device_id=me.row_peers()[i][1],
            device_id_type=MESH,
        )

    @pl.when(me.row == 0)
    def _():
        for i in range(rows - 1):
            mark_copy(i).start()
        marks[...] = block[0, :, :RANK]

    mine_half = pl.ds(pl.multiple_of(me.at[3] * half, half), half)

    def ahead_copy(k):
        _, _, peer = me.row_before(k)
        return pltpu.make_async_remote_copy(
            src_ref=block.at[me.row, :, mine_half],
            dst_ref=block.at[me.row, :, mine_half],
            send_sem=ag_s.at[k],
            recv_sem=ag_r.at[k],
            device_id=peer,
            device_id_type=MESH,
        )

    def twin_copy(k):
        row, _, _ = me.row_before(k)
        return pltpu.make_async_remote_copy(
            src_ref=block.at[row, :, mine_half],
            dst_ref=block.at[row, :, mine_half],
            send_sem=fw_s.at[k],
            recv_sem=fw_r.at[k],
            device_id=me.twin(),
            device_id_type=MESH,
        )

    def half_copy(k):
        return pltpu.make_async_remote_copy(
            src_ref=part_other.at[k],
            dst_ref=part_twin.at[k],
            send_sem=tw_s.at[k],
            recv_sem=tw_r.at[k],
            device_id=me.twin(),
            device_id_type=MESH,
        )

    def sum_copy(k):
        _, peer, _ = me.row_before(k)
        return pltpu.make_async_remote_copy(
            src_ref=part_sum.at[k],
            dst_ref=part_in.at[me.row],
            send_sem=rs_s.at[k],
            recv_sem=rs_r.at[k],
            device_id=peer,
            device_id_type=MESH,
        )

    def ahead_start(k, carry):
        ahead_copy(k).start()
        return carry

    deep = 5
    lax.fori_loop(1, deep, ahead_start, 0)

    def slab(row, sweep=None):
        right = block[row]
        out = None
        for c, cut in enumerate(pieces):
            if sweep is not None:
                sweep.inner(c)
            kern = kernel_of(own_left[cut, :], right, scale).astype(BF16)
            some = jnp.dot(weights_bf[:, cut], kern, preferred_element_type=F32)
            out = some if out is None else out + some
        return out

    def pass_on(k):
        ahead_copy(k).wait_recv()
        twin_copy(k).start()

    def of_core(value, core):
        odd = [value[:, c * width : (c + 1) * width] for c in range(1, me.cols, 2)]
        even = [value[:, c * width : (c + 1) * width] for c in range(0, me.cols, 2)]
        return jnp.where(core == 0, jnp.concatenate(even, axis=1), jnp.concatenate(odd, axis=1))

    def slab_start(k, row, sweep=None):
        value = slab(row, sweep)
        part_mine[k] = of_core(value, me.at[3])
        part_other[k] = of_core(value, 1 - me.at[3])
        half_copy(k).start()

    def settle(k):
        half_copy(k).wait_recv()
        part_sum[k] = part_mine[k] + part_twin[k]
        sum_copy(k).start()

    def slab_step(k, carry, settles=True, sweeps=None):
        pl.when(k + deep - 1 < rows)(lambda: ahead_copy(k + deep - 1).start())
        pl.when(k + 1 < rows)(lambda: pass_on(k + 1))
        twin_copy(k).wait_recv()
        sweep = None if sweeps is None else Sweep(inverse, k - sweeps)
        slab_start(k, me.row_before(k)[0], sweep)
        if settles:
            settle(k - 1)
        if sweep is not None:
            sweep.finish()
        return carry

    slab_start(0, me.row)
    pass_on(1)
    slab_step(1, 0, settles=False)
    half_copy(0).wait_recv()
    part_in[me.row] = part_mine[0] + part_twin[0]

    @pl.when(me.row != 0)
    def _():
        mark_copy(0).wait_recv()

    marks_left = as_left(marks[...]).astype(BF16)
    sketch[...] = kernel_of(marks_left, block[me.row], scale)
    turned = (((1,), (1,)), ((), ()))
    sk = sketch[...]
    gram = lax.dot_general(sk, sk, turned, precision=HI, preferred_element_type=F32)
    gram_part[...] = gram.reshape(gram_part.shape)
    gram_in[me.row] = gram_part[me.row, me.at[3]]
    third = links.start(
        me.row_peers(), lambda r: gram_part.at[r, me.at[3]], gram_in.at[me.row]
    )
    half_sketch[...] = of_core(sk, me.at[3])
    lax.fori_loop(2, 6, slab_step, 0)
    arrive(third)
    mine = total(gram_in)
    gram_own[...] = mine
    gram_all[me.at[3], me.row] = mine
    third = links.start(me.row_peers(), lambda r: gram_own, gram_all.at[me.at[3], me.row])
    lax.fori_loop(6, 8, slab_step, 0)
    arrive(third)
    its_half = gram_all.at[me.at[3]]
    third = links.start([(0, me.twin())], lambda r: its_half, its_half)
    lax.fori_loop(8, 9, slab_step, 0)
    landmarks = kernel_of(marks_left, marks[...], scale)
    arrive(third)
    gram = jnp.concatenate([gram_all[0], gram_all[1]], axis=1).reshape(inner.shape)
    inner[...] = ridge * landmarks + gram
    inverse[...] = inner[...]
    lax.fori_loop(9, rows, lambda k, carry: slab_step(k, carry, sweeps=9), 0)

    def left_step(row, carry):
        left = as_left(block[row, :, my_lanes])
        col_left[pl.ds(pl.multiple_of(row * width, width), width), :] = left.astype(BF16)
        return carry

    lax.fori_loop(0, rows, left_step, 0)
    settle(rows - 1)
    right = block[me.row]
    sweep = Sweep(inverse, rows - 9)
    for c in range(rows * width // span):
        cut = slice(c * span, (c + 1) * span)
        sweep.inner(c)
        tile[cut, :] = kernel_of(col_left[cut, :], right, scale).astype(BF16)
    sweep.finish()
    arrive(second)

    def sum_wait(k, carry):
        sum_copy(k).wait_recv()
        return carry

    lax.fori_loop(1, rows, sum_wait, 0)
    summed = -total(part_in)
    cuts = [slice(c * width, (c + 1) * width) for c in range(me.cols)]

    def at_share(value, place, places):
        at = lax.broadcasted_iota(jnp.int32, (count, places * width), 1) // width
        return jnp.where(at == place, jnp.concatenate([value] * places, axis=1), 0.0)

    chips = me.sizes[2]
    summed = summed + at_share(total(vin), me.at[2], chips)
    for c in range(chips):
        cut_part[c] = summed[:, c * width : (c + 1) * width]
    cut_in[me.at[2]] = cut_part[me.at[2]]
    each = count // me.cols

    def sum_start(turn, value):
        for c in range(me.cols):
            proj_own[turn, c] = value[c * each : (c + 1) * each]
        proj_in[turn, me.col] = proj_own[turn, me.col]
        return links.start(
            me.col_peers(), lambda c: proj_own.at[turn, c], proj_in.at[turn, me.col]
        )

    def sum_end(turn, copies):
        arrive(copies)
        mine = total(proj_in.at[turn])
        proj_sum[turn] = mine
        proj_row[turn, me.row] = mine
        landing = proj_row.at[turn, me.row]
        arrive(links.start(me.row_peers(), lambda r: proj_sum.at[turn], landing))
        mine = total(proj_row.at[turn])
        proj_all[turn] = mine
        proj_out[turn, me.col] = mine
        landing = proj_out.at[turn, me.col]
        arrive(links.start(me.col_peers(), lambda c: proj_all.at[turn], landing))
        return jnp.concatenate([proj_out[turn, c] for c in range(me.cols)], axis=0)

    def project(vector, marks_of):
        return lax.dot_general(
            vector, marks_of[...], turned, precision=HI, preferred_element_type=F32
        )

    def precondition(vector, projected):
        def product(left, right):
            return jnp.dot(left, right[...], precision=HI, preferred_element_type=F32)

        solved = product(projected, inverse)
        solved = solved + product(projected - product(solved, inner), inverse)
        mine = sketch[:, my_lanes]
        back = jnp.dot(solved, mine, precision=HI, preferred_element_type=F32)
        return (vector - back) / ridge

    def apply(turn, vector):
        rounded = vector.astype(BF16)
        dir_own[turn] = rounded
        dir_all[turn, :, lanes(me.row, width)] = rounded
        landing = dir_all.at[turn, :, lanes(me.row, width)]
        far = links.start(me.row_peers(), lambda r: dir_own.at[turn], landing)
        dir_f32[turn] = vector
        dir_col[turn, :, my_lanes] = vector
        landing = dir_col.at[turn, :, my_lanes]
        near = links.start(me.col_peers(), lambda c: dir_f32.at[turn], landing)
        arrive(far)
        sums = jnp.dot(dir_all[turn], tile[...], preferred_element_type=F32).astype(BF16)
        for c, cut in enumerate(cuts):
            im_part[turn, c] = sums[:, cut]
        im_in[turn, me.col] = im_part[turn, me.col]
        arrive(near)
        return sums.astype(F32) + at_share(ridge * vector, me.col, me.cols)

    def apply_start(turn):
        return links.start(
            me.col_peers(), lambda c: im_part.at[turn, c], im_in.at[turn, me.col]
        )

    def apply_end(turn, copies, vector):
        arrive(copies)
        return total(im_in.at[turn]) + ridge * vector

    lane = lax.broadcasted_iota(jnp.int32, (count, 128), 1)

    def dots(*pairs):
        out = jnp.zeros((count, 128), F32)
        for i, (a, b) in enumerate(pairs):
            out = jnp.where(lane == i, jnp.sum(a * b, axis=1, keepdims=True), out)
        return out

    pad = jnp.zeros((count, 128), F32)
    going = sum_start(0, jnp.concatenate([project(summed, half_sketch), pad], axis=1))
    near = links.start(me.x_peers(), lambda c: cut_part.at[c], cut_in.at[me.at[2]])
    projected = sum_end(0, going)[:, :RANK]
    arrive(near)
    res = total(cut_in)
    direction = precondition(res, projected)
    image_part = apply(0, direction)
    scalars = dots((dir_col[0], image_part)) + dots(
        (jnp.zeros_like(res), res), (res, direction)
    )
    going = sum_start(1, jnp.concatenate([project(image_part, sketch), scalars], axis=1))
    near = apply_start(0)
    packed = sum_end(1, going)
    image = apply_end(0, near, direction)
    curve, old_rz = packed[:, RANK : RANK + 1], packed[:, RANK + 1 : RANK + 2]
    alpha = old_rz / curve
    res = res - alpha * image
    precond = precondition(res, projected - alpha * packed[:, :RANK])
    image_part = apply(1, precond)
    nothing = (jnp.zeros_like(res), res)
    scalars = dots((dir_col[1], image_part), (dir_col[0], image_part)) + dots(
        nothing, nothing, (precond, image), (res, precond)
    )
    dots_own[...] = scalars
    dots_row[me.row] = scalars
    going = links.start(me.row_peers(), lambda r: dots_own, dots_row.at[me.row])
    near = apply_start(1)
    both = [p.astype(BF16) for turn in range(2) for p in thirds(dir_col[turn])]
    both = jnp.concatenate(both, axis=0)
    for c, cut in enumerate(pieces):
        at = lax.broadcasted_iota(jnp.int32, (span, group), 0) + c * span
        chosen = jnp.where(at == local, 1.0, 0.0).astype(BF16)
        got = lax.dot_general(both, chosen, turned, preferred_element_type=F32)
        for turn in range(2):
            base = 3 * count * turn
            low = got[base + count : base + 2 * count] + got[base + 2 * count : base + 3 * count]
            moved[turn, :, cut] = got[base : base + count] + low
    image_2 = apply_end(1, near, precond)
    arrive(going)
    middle = total(dots_row)
    dots_sum[...] = middle
    dots_col[me.col] = middle
    arrive(links.start(me.col_peers(), lambda c: dots_sum, dots_col.at[me.col]))
    summed = total(dots_col)
    own_curve, cross_b, cross_a, fresh = (summed[:, i : i + 1] for i in range(4))
    beta = fresh / old_rz
    last_curve = own_curve + beta * (cross_a + cross_b) + beta * beta * curve
    step = fresh / last_curve
    residual[...] = res - step * (image_2 + beta * image)
    weights_out[...] = weights[...] + ((alpha + step * beta) * moved[0] + step * moved[1])
    links.drain()

    def drain_step(k, carry):
        ahead_copy(k).wait_send()
        twin_copy(k).wait_send()
        sum_copy(k).wait_send()
        half_copy(k).wait_send()
        return carry

    lax.fori_loop(1, rows, drain_step, 0)
    half_copy(0).wait_send()

    @pl.when(me.row == 0)
    def _():
        for i in range(rows - 1):
            mark_copy(i).wait_send()


def on_device(points, weights, targets, block_index):
    features, owned = points.shape
    count = weights.shape[0]
    rows = lax.axis_size("row_0") * lax.axis_size("row_1")
    cols = lax.axis_size("col_0") * lax.axis_size("col_1")
    group = block_index.shape[1] // rows
    width = group // cols
    depth = features + TAIL
    piece = RANK // rows // lax.axis_size("col_1")
    wide = RANK + 128

    def arrays(kind, *shapes):
        return [pltpu.VMEM(shape, kind) for shape in shapes]

    cores = lax.axis_size("col_1")
    chips = cols // cores
    half = group // cores
    each = count // cols
    scratch = [
        *arrays(BF16, (features, owned)),
        *arrays(F32, (count, owned), (count, owned)),
        *arrays(jnp.int32, (1, group)),
        *arrays(BF16, (cols, features, width)),
        *arrays(F32, (cols, count, width)),
        *arrays(BF16, (cols, features, width)),
        *arrays(F32, (cols, count, width)),
        *arrays(BF16, (depth, width), (rows, depth, group), (depth, RANK)),
        *arrays(BF16, (owned, depth), (rows * width, depth), (count, owned)),
        *arrays(F32, (RANK, group)),
        *arrays(F32, (rows, cores, piece, RANK), (rows, piece, RANK), (piece, RANK)),
        *arrays(F32, (cores, rows, piece, RANK), (RANK, RANK), (RANK, RANK)),
        *arrays(F32, *[(rows, count, half)] * 5),
        *arrays(F32, (chips, count, width), (chips, count, width)),
        *arrays(BF16, (rows * width, group)),
        *arrays(F32, (RANK, half)),
        *arrays(F32, (2, cols, each, wide), (2, cols, each, wide), (2, each, wide)),
        *arrays(F32, (2, rows, each, wide), (2, each, wide), (2, cols, each, wide)),
        *arrays(F32, (count, 128), (rows, count, 128)),
        *arrays(F32, (count, 128), (cols, count, 128)),
        *arrays(BF16, (2, count, width), (2, count, rows * width)),
        *arrays(F32, (2, count, width), (2, count, group)),
        *arrays(BF16, (2, cols, count, width), (2, cols, count, width)),
        *arrays(F32, (2, count, owned)),
    ]
    near, far = cols - 1, rows - 1
    copies = 12 * near + 7 * far + chips
    dma = pltpu.SemaphoreType.DMA
    scratch += [dma((copies,)), dma((copies,)), dma((4,)), dma((far,)), dma]
    scratch += [dma((rows,))] * 8
    return tuple(
        pl.pallas_call(
            step_kernel,
            out_shape=[
                jax.ShapeDtypeStruct((count, owned), F32),
                jax.ShapeDtypeStruct((count, width), F32),
            ],
            in_specs=[pl.BlockSpec(memory_space=pl.ANY)] * 4,
            scratch_shapes=scratch,
            compiler_params=pltpu.CompilerParams(
                vmem_limit_bytes=60 * 2**20, collective_id=0, has_side_effects=True
            ),
            name="step",
        )(points, weights, targets, block_index)
    )


def solution(mesh):
    split = Mesh(mesh.devices.reshape(4, 4, 4, 2), AXES)
    spec = P(None, AXES)
    return jax.shard_map(
        on_device,
        mesh=split,
        in_specs=(spec, spec, spec, P()),
        out_specs=(spec, spec),
        check_vma=False,
    )
```

```python
import math

import jax
import jax.numpy as jnp
from jax import lax
from jax.experimental import pallas as pl
from jax.experimental.pallas import tpu as pltpu
from jax.sharding import Mesh
from jax.sharding import PartitionSpec as P

RANK = 256
ridge = 1.0
AXES = ("row_0", "row_1", "col_0", "col_1")
MESH = pl.DeviceIdType.MESH
HI = lax.Precision.HIGHEST
F32 = jnp.float32
BF16 = jnp.bfloat16
LOG2E = math.log2(math.e)
TAIL = 16


def wrap(value, size):
    return lax.rem(value, size)


class Place:
    def __init__(self):
        self.sizes = tuple(lax.axis_size(a) for a in AXES)
        self.at = tuple(lax.axis_index(a) for a in AXES)
        ny, nz, nx, nc = self.sizes
        self.rows, self.cols = ny * nz, nx * nc
        self.row = self.at[0] * nz + self.at[1]
        self.col = self.at[2] * nc + self.at[3]
        self.device = self.row * self.cols + self.col

        def hops(step, size):
            return min(step, size - step)

        self.row_steps = sorted(
            ((a, b) for a in range(ny) for b in range(nz) if a or b),
            key=lambda s: -(hops(s[0], ny) + hops(s[1], nz)),
        )
        self.col_steps = sorted(
            ((a, b) for a in range(nx) for b in range(nc) if a or b),
            key=lambda s: -(2 * hops(s[0], nx) + s[1]),
        )

    def row_peer(self, step):
        y = wrap(self.at[0] + step[0], self.sizes[0])
        z = wrap(self.at[1] + step[1], self.sizes[1])
        return y * self.sizes[1] + z, (y, z, self.at[2], self.at[3])

    def col_peer(self, step):
        x = wrap(self.at[2] + step[0], self.sizes[2])
        c = wrap(self.at[3] + step[1], self.sizes[3])
        return x * self.sizes[3] + c, (self.at[0], self.at[1], x, c)

    def x_peers(self):
        out = []
        for step in range(1, self.sizes[2]):
            x = wrap(self.at[2] + step, self.sizes[2])
            out.append((x, (self.at[0], self.at[1], x, self.at[3])))
        return out

    def twin(self):
        return self.col_peer((0, 1))[1]

    def row_peers(self):
        return [self.row_peer(s) for s in self.row_steps]

    def col_peers(self):
        return [self.col_peer(s) for s in self.col_steps]

    def row_before(self, k):
        ny, nz = self.sizes[:2]
        steps = sorted(
            ((a, b) for a in range(ny) for b in range(nz) if a or b),
            key=lambda s: (min(s[0], ny - s[0]) + min(s[1], nz - s[1]), s),
        )
        ys = sum(a << (2 * i) for i, (a, _) in enumerate(steps))
        zs = sum(b << (2 * i) for i, (_, b) in enumerate(steps))
        ys, zs = (lax.rem(jnp.right_shift(jnp.int32(v), 2 * (k - 1)), 4) for v in (ys, zs))
        behind = (wrap(self.at[0] + ny - ys, ny), wrap(self.at[1] + nz - zs, nz))
        ahead = (wrap(self.at[0] + ys, ny), wrap(self.at[1] + zs, nz))
        return behind[0] * nz + behind[1], behind + self.at[2:], ahead + self.at[2:]

    def greet(self):
        barrier = pltpu.get_barrier_semaphore()
        for _, peer in self.row_peers() + self.col_peers():
            pl.semaphore_signal(barrier, inc=1, device_id=peer, device_id_type=MESH)

    def enter(self):
        pl.semaphore_wait(pltpu.get_barrier_semaphore(), self.rows + self.cols - 2)


class Links:
    def __init__(self, sends, recvs):
        self.sends, self.recvs, self.used, self.copies = sends, recvs, 0, []

    def start(self, peers, source, target):
        started = []
        for index, peer in peers:
            copy = pltpu.make_async_remote_copy(
                src_ref=source(index),
                dst_ref=target,
                send_sem=self.sends.at[self.used],
                recv_sem=self.recvs.at[self.used],
                device_id=peer,
                device_id_type=MESH,
            )
            copy.start()
            self.used += 1
            started.append(copy)
        self.copies += started
        return started

    def drain(self):
        for copy in self.copies:
            copy.wait_send()


def arrive(copies):
    for copy in copies:
        copy.wait_recv()


def lanes(index, width):
    return pl.ds(pl.multiple_of(index * width, width), width)


def thirds(value):
    high = value.astype(BF16).astype(F32)
    rest = value - high
    middle = rest.astype(BF16).astype(F32)
    return high, middle, (rest - middle).astype(BF16).astype(F32)


def tail_rows(values, first):
    squares = -0.5 * jnp.sum(values * values, axis=0, keepdims=True)
    parts = thirds(squares)
    shape = (TAIL, values.shape[1])
    at = lax.broadcasted_iota(jnp.int32, shape, 0)
    ones = 8 - first
    rows = jnp.where((at >= ones) & (at < ones + 3), 1.0, 0.0)
    for i in range(3):
        rows = jnp.where(at == first + i, jnp.broadcast_to(parts[i], shape), rows)
    return rows


def as_left(block):
    values = block.astype(F32)
    body = values.shape[0] - TAIL
    left = jnp.concatenate([values[:body], values[body + 8 :], values[body : body + 8]], axis=0)
    return left.T


def kernel_of(left, right, scale):
    return jnp.exp2(scale * jnp.dot(left, right, preferred_element_type=F32))


def total(ref):
    value = ref[0].astype(F32)
    for i in range(1, ref.shape[0]):
        value = value + ref[i].astype(F32)
    return value


def inverse_8(rows, lane):
    shape = (8, 128)
    sub = lax.broadcasted_iota(jnp.int32, shape, 0)
    cols = [jnp.broadcast_to(rows[:, lane + j : lane + j + 1], shape) for j in range(8)]
    for k in range(8):
        pivot = 1.0 / jnp.broadcast_to(cols[k][k : k + 1, :], shape)
        here = sub == k
        column = cols[k]
        for j in range(8):
            if j != k:
                factor = jnp.broadcast_to(cols[j][k : k + 1, :], shape) * pivot
                cols[j] = jnp.where(here, factor, cols[j] - column * factor)
        cols[k] = jnp.where(here, pivot, -column * pivot)
    return cols


def sweep_8(rows, b):
    shape = (8, 128)
    rows = list(rows)
    lane = lax.broadcasted_iota(jnp.int32, shape, 1)
    sub = lax.broadcasted_iota(jnp.int32, shape, 0)
    cols = inverse_8(rows[b], 8 * b)
    inside = (lane >= 8 * b) & (lane < 8 * b + 8)
    right = jnp.where(inside, (lane - 8 * b == sub).astype(F32), rows[b])
    new = None
    for j in range(8):
        term = cols[j] * jnp.broadcast_to(right[j : j + 1, :], shape)
        new = term if new is None else new + term
    spread = [jnp.broadcast_to(new[j : j + 1, :], shape) for j in range(8)]
    for i in range(4):
        if i != b:
            acc = None
            for j in range(8):
                at = 8 * b + j
                term = jnp.broadcast_to(rows[i][:, at : at + 1], shape) * spread[j]
                acc = term if acc is None else acc + term
            rows[i] = jnp.where(inside, 0.0, rows[i]) - acc
    rows[b] = new
    return rows


class Sweep:
    def __init__(self, matrix, k, keep):
        self.matrix, self.keep, self.at = matrix, keep, pl.multiple_of(k * 32, 32)

    def inner(self, b):
        if b == 0:
            size = self.matrix.shape[0]
            rows = self.matrix[pl.ds(self.at, 32), :]
            block = pltpu.roll(rows, lax.rem(size - self.at, size), 1)[:, :128]
            self.small = [block[8 * i : 8 * i + 8, :] for i in range(4)]
        self.small = sweep_8(self.small, b)
        if b == 3:
            self.keep[...] = jnp.concatenate(self.small, axis=0)

    def finish(self):
        matrix, at, size = self.matrix, self.at, self.matrix.shape[0]
        rows = matrix[pl.ds(at, 32), :]
        lane = lax.broadcasted_iota(jnp.int32, (32, size), 1)
        sub = lax.broadcasted_iota(jnp.int32, (32, size), 0)
        wide = lax.broadcasted_iota(jnp.int32, (size, size), 1)
        inv = self.keep[:, :32]
        inside = (lane >= at) & (lane < at + 32)
        right = jnp.where(inside, (lane - at == sub).astype(F32), rows)
        new = jnp.dot(inv, right, precision=HI, preferred_element_type=F32)
        left = jnp.where(lane < at, -rows, rows)
        update = lax.dot_general(
            left, new, (((0,), (0,)), ((), ())), precision=HI, preferred_element_type=F32
        )
        matrix[...] = jnp.where((wide >= at) & (wide < at + 32), 0.0, matrix[...]) - update
        matrix[pl.ds(at, 32), :] = new


def step_kernel(points_in, weights_in, targets_in, index_in, weights_out, residual, *scratch):
    (
        points, weights, targets, index,
        piece, vpiece, pin, vin, share, block, marks,
        own_left, col_left, weights_bf, sketch,
        gram_part, gram_in, gram_own, gram_all, inner, inverse, keep,
        part_mine, part_other, part_twin, part_sum, part_in, cut_part, cut_in, tile,
        half_sketch, proj_own, proj_in, proj_sum, proj_row, proj_all, proj_out,
        dots_own, dots_row, dots_sum, dots_col,
        vec_own, vec_all, vec_col, dir_col, im_part, im_in, moved,
        col_right, col_sketch, pair,
        sends, recvs, loads, mark_s, mark_r, ag_s, ag_r, fw_s, fw_r, rs_s, rs_r, tw_s, tw_r,
    ) = scratch
    me = Place()
    rows, _, group = block.shape
    here = index_in.at[:, lanes(me.row, group)]
    pairs = [(points_in, points), (here, index), (targets_in, targets), (weights_in, weights)]
    taken = [pltpu.make_async_copy(a, b, loads.at[i]) for i, (a, b) in enumerate(pairs)]
    for copy in taken:
        copy.start()
    me.greet()
    links = Links(sends, recvs)
    for copy in taken:
        copy.wait()
    features, owned = points.shape
    count = weights.shape[0]
    width = group // me.cols
    half = group // 2
    span = min(512, owned)
    scale = 4.0 / features * LOG2E
    pieces = [slice(c * span, (c + 1) * span) for c in range(owned // span)]
    my_lanes = lanes(me.col, width)

    local = index[...] - me.device * owned
    own = targets[...] - ridge * weights[...]
    own = [p.astype(BF16) for p in thirds(own)]
    acc = None
    for c, cut in enumerate(pieces):
        at = lax.broadcasted_iota(jnp.int32, (span, group), 0) + c * span
        chosen = jnp.where(at == local, 1.0, 0.0).astype(BF16)
        left = jnp.concatenate([points[:, cut]] + [p[:, cut] for p in own], axis=0)
        some = jnp.dot(left, chosen, preferred_element_type=F32)
        acc = some if acc is None else acc + some
    for c in range(me.cols):
        cut = slice(c * width, (c + 1) * width)
        piece[c] = acc[:features, cut].astype(BF16)
        parts = acc[features:, cut]
        vpiece[c] = parts[:count] + (parts[count : 2 * count] + parts[2 * count :])
    me.enter()
    first = links.start(me.col_peers(), lambda c: piece.at[c], pin.at[me.col])
    pin[me.col] = piece[me.col]
    vin[me.col] = vpiece[me.col]
    for cut in pieces:
        some = points[:, cut].astype(F32)
        left = jnp.concatenate([some, tail_rows(some, 8)], axis=0)
        own_left[cut, :] = left.T.astype(BF16)
    weights_bf[...] = weights[...].astype(BF16)
    arrive(first)
    mine = total(pin)
    mine = jnp.concatenate([mine, tail_rows(mine, 0)], axis=0).astype(BF16)
    share[...] = mine
    block[me.row, :, my_lanes] = mine
    first = links.start(me.col_peers(), lambda c: share, block.at[me.row, :, my_lanes])
    second = links.start(me.col_peers(), lambda c: vpiece.at[c], vin.at[me.col])
    arrive(first)

    def mark_copy(i):
        return pltpu.make_async_remote_copy(
            src_ref=block.at[0, :, pl.ds(0, RANK)],
            dst_ref=marks,
            send_sem=mark_s.at[i],
            recv_sem=mark_r,
            device_id=me.row_peers()[i][1],
            device_id_type=MESH,
        )

    @pl.when(me.row == 0)
    def _():
        for i in range(rows - 1):
            mark_copy(i).start()
        marks[...] = block[0, :, :RANK]

    mine_half = pl.ds(pl.multiple_of(me.at[3] * half, half), half)

    def ahead_copy(k):
        _, _, peer = me.row_before(k)
        return pltpu.make_async_remote_copy(
            src_ref=block.at[me.row, :, mine_half],
            dst_ref=block.at[me.row, :, mine_half],
            send_sem=ag_s.at[k],
            recv_sem=ag_r.at[k],
            device_id=peer,
            device_id_type=MESH,
        )

    def twin_copy(k):
        row, _, _ = me.row_before(k)
        return pltpu.make_async_remote_copy(
            src_ref=block.at[row, :, mine_half],
            dst_ref=block.at[row, :, mine_half],
            send_sem=fw_s.at[k],
            recv_sem=fw_r.at[k],
            device_id=me.twin(),
            device_id_type=MESH,
        )

    def half_copy(k):
        return pltpu.make_async_remote_copy(
            src_ref=part_other.at[k],
            dst_ref=part_twin.at[k],
            send_sem=tw_s.at[k],
            recv_sem=tw_r.at[k],
            device_id=me.twin(),
            device_id_type=MESH,
        )

    def sum_copy(k):
        _, peer, _ = me.row_before(k)
        return pltpu.make_async_remote_copy(
            src_ref=part_sum.at[k],
            dst_ref=part_in.at[me.row],
            send_sem=rs_s.at[k],
            recv_sem=rs_r.at[k],
            device_id=peer,
            device_id_type=MESH,
        )

    def ahead_start(k, carry):
        ahead_copy(k).start()
        return carry

    deep = 5
    lax.fori_loop(1, deep, ahead_start, 0)

    def beside(piece, sweep, last):
        if piece == 0 and last is not None:
            last.finish()
        if piece > 0 and sweep is not None:
            sweep.inner(piece - 1)

    def slab(row, sweep=None, last=None):
        right = block[row]
        out = None
        for c, cut in enumerate(pieces):
            beside(c, sweep, last)
            kern = kernel_of(own_left[cut, :], right, scale).astype(BF16)
            some = jnp.dot(weights_bf[:, cut], kern, preferred_element_type=F32)
            out = some if out is None else out + some
        beside(len(pieces), sweep, last)
        mine = block[row, :, my_lanes]
        col_right[:, lanes(row, width)] = mine
        left = as_left(mine)
        col_left[pl.ds(pl.multiple_of(row * width, width), width), :] = left.astype(BF16)
        return out

    def pass_on(k):
        ahead_copy(k).wait_recv()
        twin_copy(k).start()

    def of_core(value, core):
        odd = [value[:, c * width : (c + 1) * width] for c in range(1, me.cols, 2)]
        even = [value[:, c * width : (c + 1) * width] for c in range(0, me.cols, 2)]
        return jnp.where(core == 0, jnp.concatenate(even, axis=1), jnp.concatenate(odd, axis=1))

    def slab_start(k, row, sweep=None, last=None):
        value = slab(row, sweep, last)
        part_mine[k] = of_core(value, me.at[3])
        part_other[k] = of_core(value, 1 - me.at[3])
        half_copy(k).start()

    def settle(k):
        half_copy(k).wait_recv()
        part_sum[k] = part_mine[k] + part_twin[k]
        sum_copy(k).start()

    def slab_step(k, carry, settles=True, sweeps=None, ends=False):
        pl.when(k + deep - 1 < rows)(lambda: ahead_copy(k + deep - 1).start())
        pl.when(k + 1 < rows)(lambda: pass_on(k + 1))
        twin_copy(k).wait_recv()
        sweep = None if sweeps is None else Sweep(inverse, k - sweeps, keep)
        last = Sweep(inverse, k - sweeps - 1, keep) if ends else None
        slab_start(k, me.row_before(k)[0], sweep, last)
        if settles:
            settle(k - 1)
        return carry

    slab_start(0, me.row)

    @pl.when(me.row != 0)
    def _():
        mark_copy(0).wait_recv()

    pass_on(1)
    marks_left = as_left(marks[...]).astype(BF16)
    sketch[...] = kernel_of(marks_left, block[me.row], scale)
    turned = (((1,), (1,)), ((), ()))
    sk = sketch[...]
    gram = lax.dot_general(sk, sk, turned, precision=HI, preferred_element_type=F32)
    gram_part[...] = gram.reshape(gram_part.shape)
    gram_in[me.row] = gram_part[me.row, me.at[3]]
    third = links.start(
        me.row_peers(), lambda r: gram_part.at[r, me.at[3]], gram_in.at[me.row]
    )
    half_sketch[...] = of_core(sk, me.at[3])
    slab_step(1, 0, settles=False)
    half_copy(0).wait_recv()
    part_in[me.row] = part_mine[0] + part_twin[0]
    lax.fori_loop(2, 5, slab_step, 0)
    arrive(third)
    mine = total(gram_in)
    gram_own[...] = mine
    gram_all[me.at[3], me.row] = mine
    third = links.start(me.row_peers(), lambda r: gram_own, gram_all.at[me.at[3], me.row])
    lax.fori_loop(5, 8, slab_step, 0)
    arrive(third)
    its_half = gram_all.at[me.at[3]]
    third = links.start([(0, me.twin())], lambda r: its_half, its_half)
    lax.fori_loop(8, 9, slab_step, 0)
    landmarks = kernel_of(marks_left, marks[...], scale)
    arrive(third)
    gram = jnp.concatenate([gram_all[0], gram_all[1]], axis=1).reshape(inner.shape)
    inner[...] = ridge * landmarks + gram
    inverse[...] = inner[...]
    slab_step(9, 0, sweeps=9)
    lax.fori_loop(10, rows, lambda k, carry: slab_step(k, carry, sweeps=9, ends=True), 0)

    right = block[me.row]
    sweep, last = Sweep(inverse, rows - 9, keep), Sweep(inverse, rows - 10, keep)
    parts = rows * width // span
    for c in range(parts):
        cut = slice(c * span, (c + 1) * span)
        beside(c, sweep, last)
        tile[cut, :] = kernel_of(col_left[cut, :], right, scale).astype(BF16)
        if c == 0:
            settle(rows - 1)
    beside(parts, sweep, last)
    sweep.finish()

    parts = thirds(kernel_of(marks_left, col_right[...], scale))
    for i, some in enumerate(parts):
        col_sketch[i * RANK : (i + 1) * RANK, :] = some.astype(BF16)
    step = group // 4
    for c in range(4):
        cut = slice(c * step, (c + 1) * step)
        got = jnp.dot(col_sketch[...], tile[:, cut], preferred_element_type=F32)
        got = got[:RANK] + (got[RANK : 2 * RANK] + got[2 * RANK :])
        for i, some in enumerate(thirds(got)):
            pair[i, :, cut] = some.astype(BF16)
    for i, some in enumerate(thirds(sketch[...])):
        pair[i, :, group:] = some.astype(BF16)
    arrive(second)

    def sum_wait(k, carry):
        sum_copy(k).wait_recv()
        return carry

    lax.fori_loop(1, rows, sum_wait, 0)
    summed = -total(part_in)
    cuts = [slice(c * width, (c + 1) * width) for c in range(me.cols)]

    def at_share(value, place, places):
        at = lax.broadcasted_iota(jnp.int32, (count, places * width), 1) // width
        return jnp.where(at == place, jnp.concatenate([value] * places, axis=1), 0.0)

    def of_share(value):
        at = lax.broadcasted_iota(jnp.int32, (count, group), 1) // width
        return jnp.where(at == me.col, value, 0.0)

    chips = me.sizes[2]
    summed = summed + at_share(total(vin), me.at[2], chips)
    for c in range(chips):
        cut_part[c] = summed[:, c * width : (c + 1) * width]
    cut_in[me.at[2]] = cut_part[me.at[2]]
    each = count // me.cols

    def sum_start(turn, value):
        for c in range(me.cols):
            proj_own[turn, c] = value[c * each : (c + 1) * each]
        proj_in[turn, me.col] = proj_own[turn, me.col]
        return links.start(
            me.col_peers(), lambda c: proj_own.at[turn, c], proj_in.at[turn, me.col]
        )

    def sum_rows(turn, copies):
        arrive(copies)
        mine = total(proj_in.at[turn])
        proj_sum[turn] = mine
        proj_row[turn, me.row] = mine
        landing = proj_row.at[turn, me.row]
        return links.start(me.row_peers(), lambda r: proj_sum.at[turn], landing)

    def sum_back(turn, copies):
        arrive(copies)
        mine = total(proj_row.at[turn])
        proj_all[turn] = mine
        proj_out[turn, me.col] = mine
        landing = proj_out.at[turn, me.col]
        return links.start(me.col_peers(), lambda c: proj_all.at[turn], landing)

    def sum_end(turn, copies):
        arrive(copies)
        return jnp.concatenate([proj_out[turn, c] for c in range(me.cols)], axis=0)

    def project(vector, marks_of):
        return lax.dot_general(
            vector, marks_of[...], turned, precision=HI, preferred_element_type=F32
        )

    def project_pair(vector):
        parts = [p.astype(BF16) for p in thirds(vector)]
        out = []
        for i in range(3):
            left = jnp.concatenate(parts[: 3 - i], axis=0)
            right = pair[i, :, group:]
            got = lax.dot_general(left, right, turned, preferred_element_type=F32)
            out.append([got[j * count : (j + 1) * count] for j in range(3 - i)])
        return out[0][0] + ((out[0][1] + out[1][0]) + (out[0][2] + (out[1][1] + out[2][0])))

    def solve(projected):
        def product(left, right):
            return jnp.dot(left, right[...], precision=HI, preferred_element_type=F32)

        solved = product(projected, inverse)
        return solved + product(projected - product(solved, inner), inverse)

    def times_pair(vector):
        parts = [p.astype(BF16) for p in thirds(vector)]
        out = []
        for i in range(3):
            left = jnp.concatenate(parts[: 3 - i], axis=0)
            got = jnp.dot(left, pair[i], preferred_element_type=F32)
            out.append([got[j * count : (j + 1) * count] for j in range(3 - i)])
        got = out[0][0] + ((out[0][1] + out[1][0]) + (out[0][2] + (out[1][1] + out[2][0])))
        return got[:, :group], got[:, group:]

    def spread(turn, value):
        vec_own[turn] = value
        vec_all[turn, me.row] = value
        far = links.start(me.row_peers(), lambda r: vec_own.at[turn], vec_all.at[turn, me.row])
        vec_col[turn, :, my_lanes] = value
        landing = vec_col.at[turn, :, my_lanes]
        return far, links.start(me.col_peers(), lambda c: vec_own.at[turn], landing)

    def block_times(turn):
        value = jnp.concatenate([vec_all[turn, r] for r in range(rows)], axis=1)
        value = jnp.concatenate([p.astype(BF16) for p in thirds(value)], axis=0)
        got = jnp.dot(value, tile[...], preferred_element_type=F32)
        return got[:count] + (got[count : 2 * count] + got[2 * count :])

    def image_start(turn, value):
        for c, cut in enumerate(cuts):
            im_part[turn, c] = value[:, cut]
        im_in[turn, me.col] = im_part[turn, me.col]
        return links.start(
            me.col_peers(), lambda c: im_part.at[turn, c], im_in.at[turn, me.col]
        )

    def image_end(turn, copies):
        arrive(copies)
        return total(im_in.at[turn])

    lane = lax.broadcasted_iota(jnp.int32, (count, 128), 1)

    def dots(*pairs):
        out = jnp.zeros((count, 128), F32)
        for i, (a, b) in enumerate(pairs):
            out = jnp.where(lane == i, jnp.sum(a * b, axis=1, keepdims=True), out)
        return out

    pad = jnp.zeros((count, 128), F32)
    going = sum_start(0, jnp.concatenate([project(summed, half_sketch), pad], axis=1))
    near = links.start(me.x_peers(), lambda c: cut_part.at[c], cut_in.at[me.at[2]])
    going = sum_rows(0, going)
    arrive(near)
    res = total(cut_in)
    far, near = spread(0, res)
    going = sum_back(0, going)
    arrive(far)
    block_res = block_times(0)
    arrive(near)
    res_row = vec_col[0]
    projected = sum_end(0, going)[:, :RANK]
    image_part, back = times_pair(solve(projected))
    direction = (res_row - back) / ridge
    dir_col[0] = direction
    image_part = (block_res - image_part) / ridge + of_share(ridge * direction)
    scalars = dots((direction, image_part), (of_share(direction), res_row))
    going = sum_start(1, jnp.concatenate([project_pair(image_part), scalars], axis=1))
    near = image_start(0, image_part)
    going = sum_rows(1, going)
    image = image_end(0, near)
    far, near = spread(1, image)
    going = sum_back(1, going)
    arrive(far)
    block_image = block_times(1)
    arrive(near)
    image_row = vec_col[1]
    packed = sum_end(1, going)
    curve, old_rz = packed[:, RANK : RANK + 1], packed[:, RANK + 1 : RANK + 2]
    alpha = old_rz / curve
    res = res - alpha * image
    res_row = res_row - alpha * image_row
    image_part, back = times_pair(solve(projected - alpha * packed[:, :RANK]))
    precond = (res_row - back) / ridge
    dir_col[1] = precond
    image_part = (block_res - alpha * block_image - image_part) / ridge
    image_part = image_part + of_share(ridge * precond)
    mine = of_share(precond)
    scalars = dots(
        (precond, image_part), (direction, image_part), (mine, image_row), (mine, res_row)
    )
    dots_own[...] = scalars
    dots_row[me.row] = scalars
    going = links.start(me.row_peers(), lambda r: dots_own, dots_row.at[me.row])
    near = image_start(1, image_part)
    both = [p.astype(BF16) for turn in range(2) for p in thirds(dir_col[turn])]
    both = jnp.concatenate(both, axis=0)
    for c, cut in enumerate(pieces):
        at = lax.broadcasted_iota(jnp.int32, (span, group), 0) + c * span
        chosen = jnp.where(at == local, 1.0, 0.0).astype(BF16)
        got = lax.dot_general(both, chosen, turned, preferred_element_type=F32)
        for turn in range(2):
            base = 3 * count * turn
            low = got[base + count : base + 2 * count] + got[base + 2 * count : base + 3 * count]
            moved[turn, :, cut] = got[base : base + count] + low
    image_2 = image_end(1, near)
    arrive(going)
    middle = total(dots_row)
    dots_sum[...] = middle
    dots_col[me.col] = middle
    arrive(links.start(me.col_peers(), lambda c: dots_sum, dots_col.at[me.col]))
    summed = total(dots_col)
    own_curve, cross_b, cross_a, fresh = (summed[:, i : i + 1] for i in range(4))
    beta = fresh / old_rz
    last_curve = own_curve + beta * (cross_a + cross_b) + beta * beta * curve
    step = fresh / last_curve
    residual[...] = res - step * (image_2 + beta * image)
    weights_out[...] = weights[...] + ((alpha + step * beta) * moved[0] + step * moved[1])
    links.drain()

    def drain_step(k, carry):
        ahead_copy(k).wait_send()
        twin_copy(k).wait_send()
        sum_copy(k).wait_send()
        half_copy(k).wait_send()
        return carry

    lax.fori_loop(1, rows, drain_step, 0)
    half_copy(0).wait_send()

    @pl.when(me.row == 0)
    def _():
        for i in range(rows - 1):
            mark_copy(i).wait_send()


def on_device(points, weights, targets, block_index):
    features, owned = points.shape
    count = weights.shape[0]
    rows = lax.axis_size("row_0") * lax.axis_size("row_1")
    cols = lax.axis_size("col_0") * lax.axis_size("col_1")
    group = block_index.shape[1] // rows
    width = group // cols
    depth = features + TAIL
    piece = RANK // rows // lax.axis_size("col_1")
    wide = RANK + 128

    def arrays(kind, *shapes):
        return [pltpu.VMEM(shape, kind) for shape in shapes]

    cores = lax.axis_size("col_1")
    chips = cols // cores
    half = group // cores
    each = count // cols
    scratch = [
        *arrays(BF16, (features, owned)),
        *arrays(F32, (count, owned), (count, owned)),
        *arrays(jnp.int32, (1, group)),
        *arrays(BF16, (cols, features, width)),
        *arrays(F32, (cols, count, width)),
        *arrays(BF16, (cols, features, width)),
        *arrays(F32, (cols, count, width)),
        *arrays(BF16, (depth, width), (rows, depth, group), (depth, RANK)),
        *arrays(BF16, (owned, depth), (rows * width, depth), (count, owned)),
        *arrays(F32, (RANK, group)),
        *arrays(F32, (rows, cores, piece, RANK), (rows, piece, RANK), (piece, RANK)),
        *arrays(F32, (cores, rows, piece, RANK), (RANK, RANK), (RANK, RANK), (32, 128)),
        *arrays(F32, *[(rows, count, half)] * 5),
        *arrays(F32, (chips, count, width), (chips, count, width)),
        *arrays(BF16, (rows * width, group)),
        *arrays(F32, (RANK, half)),
        *arrays(F32, (2, cols, each, wide), (2, cols, each, wide), (2, each, wide)),
        *arrays(F32, (2, rows, each, wide), (2, each, wide), (2, cols, each, wide)),
        *arrays(F32, (count, 128), (rows, count, 128)),
        *arrays(F32, (count, 128), (cols, count, 128)),
        *arrays(F32, (2, count, width), (2, rows, count, width)),
        *arrays(F32, (2, count, group), (2, count, group)),
        *arrays(F32, (2, cols, count, width), (2, cols, count, width)),
        *arrays(F32, (2, count, owned)),
        *arrays(BF16, (depth, rows * width), (3 * RANK, rows * width)),
        *arrays(BF16, (3, RANK, 2 * group)),
    ]
    near, far = cols - 1, rows - 1
    copies = 12 * near + 7 * far + chips
    dma = pltpu.SemaphoreType.DMA
    scratch += [dma((copies,)), dma((copies,)), dma((4,)), dma((far,)), dma]
    scratch += [dma((rows,))] * 8
    return tuple(
        pl.pallas_call(
            step_kernel,
            out_shape=[
                jax.ShapeDtypeStruct((count, owned), F32),
                jax.ShapeDtypeStruct((count, width), F32),
            ],
            in_specs=[pl.BlockSpec(memory_space=pl.ANY)] * 4,
            scratch_shapes=scratch,
            compiler_params=pltpu.CompilerParams(
                vmem_limit_bytes=60 * 2**20, collective_id=0, has_side_effects=True
            ),
            name="step",
        )(points, weights, targets, block_index)
    )


def solution(mesh):
    split = Mesh(mesh.devices.reshape(4, 4, 4, 2), AXES)
    spec = P(None, AXES)
    return jax.shard_map(
        on_device,
        mesh=split,
        in_specs=(spec, spec, spec, P()),
        out_specs=(spec, spec),
        check_vma=False,
    )
```

```python
import math

import jax
import jax.numpy as jnp
from jax import lax
from jax.experimental import pallas as pl
from jax.experimental.pallas import tpu as pltpu
from jax.sharding import Mesh
from jax.sharding import PartitionSpec as P

RANK = 256
ridge = 1.0
AXES = ("row_0", "row_1", "col_0", "col_1")
MESH = pl.DeviceIdType.MESH
HI = lax.Precision.HIGHEST
F32 = jnp.float32
BF16 = jnp.bfloat16
LOG2E = math.log2(math.e)
TAIL = 16


def wrap(value, size):
    return lax.rem(value, size)


class Place:
    def __init__(self):
        self.sizes = tuple(lax.axis_size(a) for a in AXES)
        self.at = tuple(lax.axis_index(a) for a in AXES)
        ny, nz, nx, nc = self.sizes
        self.rows, self.cols = ny * nz, nx * nc
        self.row = self.at[0] * nz + self.at[1]
        self.col = self.at[2] * nc + self.at[3]
        self.device = self.row * self.cols + self.col

        def hops(step, size):
            return min(step, size - step)

        self.row_steps = sorted(
            ((a, b) for a in range(ny) for b in range(nz) if a or b),
            key=lambda s: -(hops(s[0], ny) + hops(s[1], nz)),
        )
        self.col_steps = sorted(
            ((a, b) for a in range(nx) for b in range(nc) if a or b),
            key=lambda s: -(2 * hops(s[0], nx) + s[1]),
        )

    def row_peer(self, step):
        y = wrap(self.at[0] + step[0], self.sizes[0])
        z = wrap(self.at[1] + step[1], self.sizes[1])
        return y * self.sizes[1] + z, (y, z, self.at[2], self.at[3])

    def col_peer(self, step):
        x = wrap(self.at[2] + step[0], self.sizes[2])
        c = wrap(self.at[3] + step[1], self.sizes[3])
        return x * self.sizes[3] + c, (self.at[0], self.at[1], x, c)

    def x_peers(self):
        out = []
        for step in range(1, self.sizes[2]):
            x = wrap(self.at[2] + step, self.sizes[2])
            out.append((x, (self.at[0], self.at[1], x, self.at[3])))
        return out

    def twin(self):
        return self.col_peer((0, 1))[1]

    def row_peers(self):
        return [self.row_peer(s) for s in self.row_steps]

    def col_peers(self):
        return [self.col_peer(s) for s in self.col_steps]

    def row_before(self, k):
        ny, nz = self.sizes[:2]
        steps = sorted(
            ((a, b) for a in range(ny) for b in range(nz) if a or b),
            key=lambda s: (min(s[0], ny - s[0]) + min(s[1], nz - s[1]), s),
        )
        ys = sum(a << (2 * i) for i, (a, _) in enumerate(steps))
        zs = sum(b << (2 * i) for i, (_, b) in enumerate(steps))
        ys, zs = (lax.rem(jnp.right_shift(jnp.int32(v), 2 * (k - 1)), 4) for v in (ys, zs))
        behind = (wrap(self.at[0] + ny - ys, ny), wrap(self.at[1] + nz - zs, nz))
        ahead = (wrap(self.at[0] + ys, ny), wrap(self.at[1] + zs, nz))
        return behind[0] * nz + behind[1], behind + self.at[2:], ahead + self.at[2:]

    def greet(self):
        barrier = pltpu.get_barrier_semaphore()
        for _, peer in self.row_peers() + self.col_peers():
            pl.semaphore_signal(barrier, inc=1, device_id=peer, device_id_type=MESH)

    def enter(self):
        pl.semaphore_wait(pltpu.get_barrier_semaphore(), self.rows + self.cols - 2)


class Links:
    def __init__(self, sends, recvs):
        self.sends, self.recvs, self.wholes = sends, recvs, []

    def start(self, peers, source, target, whole):
        at = len(self.wholes)
        self.wholes.append(whole)
        for index, peer in peers:
            pltpu.make_async_remote_copy(
                src_ref=source(index),
                dst_ref=target,
                send_sem=self.sends.at[at],
                recv_sem=self.recvs.at[at],
                device_id=peer,
                device_id_type=MESH,
            ).start()
        return whole, self.recvs.at[at]

    def drain(self):
        for at, whole in enumerate(self.wholes):
            arrive((whole, self.sends.at[at]))


def arrive(exchange):
    whole, semaphore = exchange
    pltpu.make_async_copy(whole, whole, semaphore).wait()


def head(ref, length):
    return ref.at[pl.ds(0, length)]


def lanes(index, width):
    return pl.ds(pl.multiple_of(index * width, width), width)


def thirds(value):
    high = value.astype(BF16).astype(F32)
    rest = value - high
    middle = rest.astype(BF16).astype(F32)
    return high, middle, (rest - middle).astype(BF16).astype(F32)


def tail_rows(values, first):
    squares = -0.5 * jnp.sum(values * values, axis=0, keepdims=True)
    parts = thirds(squares)
    shape = (TAIL, values.shape[1])
    at = lax.broadcasted_iota(jnp.int32, shape, 0)
    ones = 8 - first
    rows = jnp.where((at >= ones) & (at < ones + 3), 1.0, 0.0)
    for i in range(3):
        rows = jnp.where(at == first + i, jnp.broadcast_to(parts[i], shape), rows)
    return rows


def as_left(block):
    values = block.astype(F32)
    body = values.shape[0] - TAIL
    left = jnp.concatenate([values[:body], values[body + 8 :], values[body : body + 8]], axis=0)
    return left.T


def kernel_of(left, right, scale):
    return jnp.exp2(scale * jnp.dot(left, right, preferred_element_type=F32))


def total(ref):
    value = ref[0].astype(F32)
    for i in range(1, ref.shape[0]):
        value = value + ref[i].astype(F32)
    return value


def inverse_8(rows, lane):
    shape = (8, 128)
    sub = lax.broadcasted_iota(jnp.int32, shape, 0)
    cols = [jnp.broadcast_to(rows[:, lane + j : lane + j + 1], shape) for j in range(8)]
    for k in range(8):
        pivot = 1.0 / jnp.broadcast_to(cols[k][k : k + 1, :], shape)
        here = sub == k
        column = cols[k]
        for j in range(8):
            if j != k:
                factor = jnp.broadcast_to(cols[j][k : k + 1, :], shape) * pivot
                cols[j] = jnp.where(here, factor, cols[j] - column * factor)
        cols[k] = jnp.where(here, pivot, -column * pivot)
    return cols


def sweep_8(rows, b):
    shape = (8, 128)
    rows = list(rows)
    lane = lax.broadcasted_iota(jnp.int32, shape, 1)
    sub = lax.broadcasted_iota(jnp.int32, shape, 0)
    cols = inverse_8(rows[b], 8 * b)
    inside = (lane >= 8 * b) & (lane < 8 * b + 8)
    right = jnp.where(inside, (lane - 8 * b == sub).astype(F32), rows[b])
    new = None
    for j in range(8):
        term = cols[j] * jnp.broadcast_to(right[j : j + 1, :], shape)
        new = term if new is None else new + term
    spread = [jnp.broadcast_to(new[j : j + 1, :], shape) for j in range(8)]
    for i in range(4):
        if i != b:
            acc = None
            for j in range(8):
                at = 8 * b + j
                term = jnp.broadcast_to(rows[i][:, at : at + 1], shape) * spread[j]
                acc = term if acc is None else acc + term
            rows[i] = jnp.where(inside, 0.0, rows[i]) - acc
    rows[b] = new
    return rows


class Sweep:
    def __init__(self, matrix, k, keep):
        self.matrix, self.keep, self.at = matrix, keep, pl.multiple_of(k * 32, 32)

    def inner(self, b):
        if b == 0:
            size = self.matrix.shape[0]
            rows = self.matrix[pl.ds(self.at, 32), :]
            block = pltpu.roll(rows, lax.rem(size - self.at, size), 1)[:, :128]
            self.small = [block[8 * i : 8 * i + 8, :] for i in range(4)]
        self.small = sweep_8(self.small, b)
        if b == 3:
            self.keep[...] = jnp.concatenate(self.small, axis=0)

    def finish(self):
        matrix, at, size = self.matrix, self.at, self.matrix.shape[0]
        rows = matrix[pl.ds(at, 32), :]
        lane = lax.broadcasted_iota(jnp.int32, (32, size), 1)
        sub = lax.broadcasted_iota(jnp.int32, (32, size), 0)
        wide = lax.broadcasted_iota(jnp.int32, (size, size), 1)
        inv = self.keep[:, :32]
        inside = (lane >= at) & (lane < at + 32)
        right = jnp.where(inside, (lane - at == sub).astype(F32), rows)
        new = jnp.dot(inv, right, precision=HI, preferred_element_type=F32)
        left = jnp.where(lane < at, -rows, rows)
        update = lax.dot_general(
            left, new, (((0,), (0,)), ((), ())), precision=HI, preferred_element_type=F32
        )
        matrix[...] = jnp.where((wide >= at) & (wide < at + 32), 0.0, matrix[...]) - update
        matrix[pl.ds(at, 32), :] = new


def step_kernel(points_in, weights_in, targets_in, index_in, weights_out, residual, *scratch):
    (
        points, weights, targets, index,
        piece, vpiece, pin, vin, share, block, marks,
        own_left, col_left, weights_bf, sketch,
        gram_part, gram_in, gram_own, gram_all, inner, inverse, keep,
        part_mine, part_other, part_twin, part_sum, part_in, cut_part, cut_in, tile,
        half_sketch, proj_own, proj_in, proj_sum, proj_row, proj_all, proj_out,
        dots_own, dots_row, dots_sum, dots_col,
        vec_own, vec_all, vec_col, dir_col, im_part, im_in, moved,
        col_right, col_sketch, pair,
        sends, recvs, loads, mark_s, mark_r, ag_s, ag_r, fw_s, fw_r, rs_s, rs_r, tw_s, tw_r,
    ) = scratch
    me = Place()
    rows, _, group = block.shape
    here = index_in.at[:, lanes(me.row, group)]
    pairs = [(points_in, points), (here, index), (targets_in, targets), (weights_in, weights)]
    taken = [pltpu.make_async_copy(a, b, loads.at[i]) for i, (a, b) in enumerate(pairs)]
    for copy in taken:
        copy.start()
    me.greet()
    links = Links(sends, recvs)
    near_count, far_count = me.cols - 1, rows - 1
    for copy in taken:
        copy.wait()
    features, owned = points.shape
    count = weights.shape[0]
    width = group // me.cols
    half = group // 2
    span = min(512, owned)
    scale = 4.0 / features * LOG2E
    pieces = [slice(c * span, (c + 1) * span) for c in range(owned // span)]
    my_lanes = lanes(me.col, width)

    local = index[...] - me.device * owned
    own = targets[...] - ridge * weights[...]
    own = [p.astype(BF16) for p in thirds(own)]
    acc = None
    for c, cut in enumerate(pieces):
        at = lax.broadcasted_iota(jnp.int32, (span, group), 0) + c * span
        chosen = jnp.where(at == local, 1.0, 0.0).astype(BF16)
        left = jnp.concatenate([points[:, cut]] + [p[:, cut] for p in own], axis=0)
        some = jnp.dot(left, chosen, preferred_element_type=F32)
        acc = some if acc is None else acc + some
    for c in range(me.cols):
        cut = slice(c * width, (c + 1) * width)
        piece[c] = acc[:features, cut].astype(BF16)
        parts = acc[features:, cut]
        vpiece[c] = parts[:count] + (parts[count : 2 * count] + parts[2 * count :])
    me.enter()
    first = links.start(
        me.col_peers(), lambda c: piece.at[c], pin.at[me.col], head(pin, near_count)
    )
    pin[me.col] = piece[me.col]
    vin[me.col] = vpiece[me.col]
    for cut in pieces:
        some = points[:, cut].astype(F32)
        left = jnp.concatenate([some, tail_rows(some, 8)], axis=0)
        own_left[cut, :] = left.T.astype(BF16)
    weights_bf[...] = weights[...].astype(BF16)
    arrive(first)
    mine = total(pin)
    mine = jnp.concatenate([mine, tail_rows(mine, 0)], axis=0).astype(BF16)
    share[...] = mine
    block[me.row, :, my_lanes] = mine
    most = block.at[me.row, :, pl.ds(0, near_count * width)]
    first = links.start(me.col_peers(), lambda c: share, block.at[me.row, :, my_lanes], most)
    second = links.start(
        me.col_peers(), lambda c: vpiece.at[c], vin.at[me.col], head(vin, near_count)
    )
    arrive(first)

    def mark_copy(i):
        return pltpu.make_async_remote_copy(
            src_ref=block.at[0, :, pl.ds(0, RANK)],
            dst_ref=marks,
            send_sem=mark_s,
            recv_sem=mark_r,
            device_id=me.row_peers()[i][1],
            device_id_type=MESH,
        )

    @pl.when(me.row == 0)
    def _():
        for i in range(rows - 1):
            mark_copy(i).start()
        marks[...] = block[0, :, :RANK]

    mine_half = pl.ds(pl.multiple_of(me.at[3] * half, half), half)

    def ahead_copy(k):
        _, _, peer = me.row_before(k)
        return pltpu.make_async_remote_copy(
            src_ref=block.at[me.row, :, mine_half],
            dst_ref=block.at[me.row, :, mine_half],
            send_sem=ag_s,
            recv_sem=ag_r.at[k],
            device_id=peer,
            device_id_type=MESH,
        )

    def twin_copy(k):
        row, _, _ = me.row_before(k)
        return pltpu.make_async_remote_copy(
            src_ref=block.at[row, :, mine_half],
            dst_ref=block.at[row, :, mine_half],
            send_sem=fw_s,
            recv_sem=fw_r.at[k],
            device_id=me.twin(),
            device_id_type=MESH,
        )

    def half_copy(k):
        return pltpu.make_async_remote_copy(
            src_ref=part_other.at[k],
            dst_ref=part_twin.at[k],
            send_sem=tw_s,
            recv_sem=tw_r.at[k],
            device_id=me.twin(),
            device_id_type=MESH,
        )

    def sum_copy(k):
        _, peer, _ = me.row_before(k)
        return pltpu.make_async_remote_copy(
            src_ref=part_sum.at[k],
            dst_ref=part_in.at[me.row],
            send_sem=rs_s,
            recv_sem=rs_r,
            device_id=peer,
            device_id_type=MESH,
        )

    def ahead_start(k, carry):
        ahead_copy(k).start()
        return carry

    deep = 5
    lax.fori_loop(1, deep, ahead_start, 0)

    def beside(piece, sweep, last):
        if piece == 0 and last is not None:
            last.finish()
        if piece > 0 and sweep is not None:
            sweep.inner(piece - 1)

    def slab(row, sweep=None, last=None):
        right = block[row]
        out = None
        for c, cut in enumerate(pieces):
            beside(c, sweep, last)
            kern = kernel_of(own_left[cut, :], right, scale).astype(BF16)
            some = jnp.dot(weights_bf[:, cut], kern, preferred_element_type=F32)
            out = some if out is None else out + some
        beside(len(pieces), sweep, last)
        mine = block[row, :, my_lanes]
        col_right[:, lanes(row, width)] = mine
        left = as_left(mine)
        col_left[pl.ds(pl.multiple_of(row * width, width), width), :] = left.astype(BF16)
        return out

    def pass_on(k):
        ahead_copy(k).wait_recv()
        twin_copy(k).start()

    def of_core(value, core):
        odd = [value[:, c * width : (c + 1) * width] for c in range(1, me.cols, 2)]
        even = [value[:, c * width : (c + 1) * width] for c in range(0, me.cols, 2)]
        return jnp.where(core == 0, jnp.concatenate(even, axis=1), jnp.concatenate(odd, axis=1))

    def slab_start(k, row, sweep=None, last=None):
        value = slab(row, sweep, last)
        part_mine[k] = of_core(value, me.at[3])
        part_other[k] = of_core(value, 1 - me.at[3])
        half_copy(k).start()

    def settle(k):
        half_copy(k).wait_recv()
        part_sum[k] = part_mine[k] + part_twin[k]
        sum_copy(k).start()

    def slab_step(k, carry, settles=True, sweeps=None, ends=False):
        pl.when(k + deep - 1 < rows)(lambda: ahead_copy(k + deep - 1).start())
        pl.when(k + 1 < rows)(lambda: pass_on(k + 1))
        twin_copy(k).wait_recv()
        sweep = None if sweeps is None else Sweep(inverse, k - sweeps, keep)
        last = Sweep(inverse, k - sweeps - 1, keep) if ends else None
        slab_start(k, me.row_before(k)[0], sweep, last)
        if settles:
            settle(k - 1)
        return carry

    slab_start(0, me.row)

    pass_on(1)
    slab_step(1, 0, settles=False)
    half_copy(0).wait_recv()
    part_in[me.row] = part_mine[0] + part_twin[0]

    @pl.when(me.row != 0)
    def _():
        mark_copy(0).wait_recv()

    marks_left = as_left(marks[...]).astype(BF16)
    sketch[...] = kernel_of(marks_left, block[me.row], scale)
    turned = (((1,), (1,)), ((), ()))
    sk = sketch[...]
    gram = lax.dot_general(sk, sk, turned, precision=HI, preferred_element_type=F32)
    gram_part[...] = gram.reshape(gram_part.shape)
    gram_in[me.row] = gram_part[me.row, me.at[3]]
    third = links.start(
        me.row_peers(),
        lambda r: gram_part.at[r, me.at[3]],
        gram_in.at[me.row],
        head(gram_in, far_count),
    )
    half_sketch[...] = of_core(sk, me.at[3])
    lax.fori_loop(2, 5, slab_step, 0)
    arrive(third)
    mine = total(gram_in)
    gram_own[...] = mine
    gram_all[me.at[3], me.row] = mine
    its_half = gram_all.at[me.at[3]]
    third = links.start(
        me.row_peers(), lambda r: gram_own, its_half.at[me.row], head(its_half, far_count)
    )
    lax.fori_loop(5, 8, slab_step, 0)
    arrive(third)
    third = links.start([(0, me.twin())], lambda r: its_half, its_half, its_half)
    lax.fori_loop(8, 9, slab_step, 0)
    landmarks = kernel_of(marks_left, marks[...], scale)
    arrive(third)
    gram = jnp.concatenate([gram_all[0], gram_all[1]], axis=1).reshape(inner.shape)
    inner[...] = ridge * landmarks + gram
    inverse[...] = inner[...]
    slab_step(9, 0, sweeps=9)
    lax.fori_loop(10, rows, lambda k, carry: slab_step(k, carry, sweeps=9, ends=True), 0)

    right = block[me.row]
    sweep, last = Sweep(inverse, rows - 9, keep), Sweep(inverse, rows - 10, keep)
    parts = rows * width // span
    for c in range(parts):
        cut = slice(c * span, (c + 1) * span)
        beside(c, sweep, last)
        tile[cut, :] = kernel_of(col_left[cut, :], right, scale).astype(BF16)
        if c == 0:
            settle(rows - 1)
    beside(parts, sweep, last)
    sweep.finish()

    parts = thirds(kernel_of(marks_left, col_right[...], scale))
    for i, some in enumerate(parts):
        col_sketch[i * RANK : (i + 1) * RANK, :] = some.astype(BF16)
    step = group // 4
    for c in range(4):
        cut = slice(c * step, (c + 1) * step)
        got = jnp.dot(col_sketch[...], tile[:, cut], preferred_element_type=F32)
        got = got[:RANK] + (got[RANK : 2 * RANK] + got[2 * RANK :])
        for i, some in enumerate(thirds(got)):
            pair[i, :, cut] = some.astype(BF16)
    for i, some in enumerate(thirds(sketch[...])):
        pair[i, :, group:] = some.astype(BF16)
    arrive(second)

    arrive((head(part_in, far_count), rs_r))
    summed = -total(part_in)
    cuts = [slice(c * width, (c + 1) * width) for c in range(me.cols)]

    def at_share(value, place, places):
        at = lax.broadcasted_iota(jnp.int32, (count, places * width), 1) // width
        return jnp.where(at == place, jnp.concatenate([value] * places, axis=1), 0.0)

    def of_share(value):
        at = lax.broadcasted_iota(jnp.int32, (count, group), 1) // width
        return jnp.where(at == me.col, value, 0.0)

    chips = me.sizes[2]
    summed = summed + at_share(total(vin), me.at[2], chips)
    for c in range(chips):
        cut_part[c] = summed[:, c * width : (c + 1) * width]
    cut_in[me.at[2]] = cut_part[me.at[2]]
    each = count // me.cols

    def sum_start(turn, value):
        for c in range(me.cols):
            proj_own[turn, c] = value[c * each : (c + 1) * each]
        proj_in[turn, me.col] = proj_own[turn, me.col]
        return links.start(
            me.col_peers(),
            lambda c: proj_own.at[turn, c],
            proj_in.at[turn, me.col],
            head(proj_in.at[turn], near_count),
        )

    def sum_rows(turn, copies):
        arrive(copies)
        mine = total(proj_in.at[turn])
        proj_sum[turn] = mine
        proj_row[turn, me.row] = mine
        landing, whole = proj_row.at[turn, me.row], head(proj_row.at[turn], far_count)
        return links.start(me.row_peers(), lambda r: proj_sum.at[turn], landing, whole)

    def sum_back(turn, copies):
        arrive(copies)
        mine = total(proj_row.at[turn])
        proj_all[turn] = mine
        proj_out[turn, me.col] = mine
        landing, whole = proj_out.at[turn, me.col], head(proj_out.at[turn], near_count)
        return links.start(me.col_peers(), lambda c: proj_all.at[turn], landing, whole)

    def sum_end(turn, copies):
        arrive(copies)
        return jnp.concatenate([proj_out[turn, c] for c in range(me.cols)], axis=0)

    def project(vector, marks_of):
        return lax.dot_general(
            vector, marks_of[...], turned, precision=HI, preferred_element_type=F32
        )

    def project_pair(vector):
        parts = [p.astype(BF16) for p in thirds(vector)]
        out = []
        for i in range(3):
            left = jnp.concatenate(parts[: 3 - i], axis=0)
            right = pair[i, :, group:]
            got = lax.dot_general(left, right, turned, preferred_element_type=F32)
            out.append([got[j * count : (j + 1) * count] for j in range(3 - i)])
        return out[0][0] + ((out[0][1] + out[1][0]) + (out[0][2] + (out[1][1] + out[2][0])))

    def solve(projected):
        def product(left, right):
            return jnp.dot(left, right[...], precision=HI, preferred_element_type=F32)

        solved = product(projected, inverse)
        return solved + product(projected - product(solved, inner), inverse)

    def times_pair(vector):
        parts = [p.astype(BF16) for p in thirds(vector)]
        out = []
        for i in range(3):
            left = jnp.concatenate(parts[: 3 - i], axis=0)
            got = jnp.dot(left, pair[i], preferred_element_type=F32)
            out.append([got[j * count : (j + 1) * count] for j in range(3 - i)])
        got = out[0][0] + ((out[0][1] + out[1][0]) + (out[0][2] + (out[1][1] + out[2][0])))
        return got[:, :group], got[:, group:]

    def spread(turn, value):
        vec_own[turn] = value
        vec_all[turn, me.row] = value
        landing, whole = vec_all.at[turn, me.row], head(vec_all.at[turn], far_count)
        far = links.start(me.row_peers(), lambda r: vec_own.at[turn], landing, whole)
        vec_col[turn, :, my_lanes] = value
        landing = vec_col.at[turn, :, my_lanes]
        whole = vec_col.at[turn, :, pl.ds(0, near_count * width)]
        return far, links.start(me.col_peers(), lambda c: vec_own.at[turn], landing, whole)

    def block_times(turn):
        value = jnp.concatenate([vec_all[turn, r] for r in range(rows)], axis=1)
        value = jnp.concatenate([p.astype(BF16) for p in thirds(value)], axis=0)
        got = jnp.dot(value, tile[...], preferred_element_type=F32)
        return got[:count] + (got[count : 2 * count] + got[2 * count :])

    def image_start(turn, value):
        for c, cut in enumerate(cuts):
            im_part[turn, c] = value[:, cut]
        im_in[turn, me.col] = im_part[turn, me.col]
        return links.start(
            me.col_peers(),
            lambda c: im_part.at[turn, c],
            im_in.at[turn, me.col],
            head(im_in.at[turn], near_count),
        )

    def image_end(turn, copies):
        arrive(copies)
        return total(im_in.at[turn])

    lane = lax.broadcasted_iota(jnp.int32, (count, 128), 1)

    def dots(*pairs):
        out = jnp.zeros((count, 128), F32)
        for i, (a, b) in enumerate(pairs):
            out = jnp.where(lane == i, jnp.sum(a * b, axis=1, keepdims=True), out)
        return out

    pad = jnp.zeros((count, 128), F32)
    going = sum_start(0, jnp.concatenate([project(summed, half_sketch), pad], axis=1))
    near = links.start(
        me.x_peers(), lambda c: cut_part.at[c], cut_in.at[me.at[2]], head(cut_in, chips - 1)
    )
    going = sum_rows(0, going)
    arrive(near)
    res = total(cut_in)
    far, near = spread(0, res)
    going = sum_back(0, going)
    arrive(far)
    block_res = block_times(0)
    arrive(near)
    res_row = vec_col[0]
    projected = sum_end(0, going)[:, :RANK]
    image_part, back = times_pair(solve(projected))
    direction = (res_row - back) / ridge
    dir_col[0] = direction
    image_part = (block_res - image_part) / ridge + of_share(ridge * direction)
    scalars = dots((direction, image_part), (of_share(direction), res_row))
    going = sum_start(1, jnp.concatenate([project_pair(image_part), scalars], axis=1))
    near = image_start(0, image_part)
    going = sum_rows(1, going)
    image = image_end(0, near)
    far, near = spread(1, image)
    going = sum_back(1, going)
    arrive(far)
    block_image = block_times(1)
    arrive(near)
    image_row = vec_col[1]
    packed = sum_end(1, going)
    curve, old_rz = packed[:, RANK : RANK + 1], packed[:, RANK + 1 : RANK + 2]
    alpha = old_rz / curve
    res = res - alpha * image
    res_row = res_row - alpha * image_row
    image_part, back = times_pair(solve(projected - alpha * packed[:, :RANK]))
    precond = (res_row - back) / ridge
    dir_col[1] = precond
    image_part = (block_res - alpha * block_image - image_part) / ridge
    image_part = image_part + of_share(ridge * precond)
    mine = of_share(precond)
    scalars = dots(
        (precond, image_part), (direction, image_part), (mine, image_row), (mine, res_row)
    )
    dots_own[...] = scalars
    dots_row[me.row] = scalars
    going = links.start(
        me.row_peers(), lambda r: dots_own, dots_row.at[me.row], head(dots_row, far_count)
    )
    near = image_start(1, image_part)
    both = [p.astype(BF16) for turn in range(2) for p in thirds(dir_col[turn])]
    both = jnp.concatenate(both, axis=0)
    for c, cut in enumerate(pieces):
        at = lax.broadcasted_iota(jnp.int32, (span, group), 0) + c * span
        chosen = jnp.where(at == local, 1.0, 0.0).astype(BF16)
        got = lax.dot_general(both, chosen, turned, preferred_element_type=F32)
        for turn in range(2):
            base = 3 * count * turn
            low = got[base + count : base + 2 * count] + got[base + 2 * count : base + 3 * count]
            moved[turn, :, cut] = got[base : base + count] + low
    image_2 = image_end(1, near)
    arrive(going)
    middle = total(dots_row)
    dots_sum[...] = middle
    dots_col[me.col] = middle
    arrive(
        links.start(
            me.col_peers(), lambda c: dots_sum, dots_col.at[me.col], head(dots_col, near_count)
        )
    )
    summed = total(dots_col)
    own_curve, cross_b, cross_a, fresh = (summed[:, i : i + 1] for i in range(4))
    beta = fresh / old_rz
    last_curve = own_curve + beta * (cross_a + cross_b) + beta * beta * curve
    step = fresh / last_curve
    residual[...] = res - step * (image_2 + beta * image)
    weights_out[...] = weights[...] + ((alpha + step * beta) * moved[0] + step * moved[1])
    links.drain()
    arrive((block.at[pl.ds(0, far_count), :, mine_half], ag_s))
    arrive((block.at[pl.ds(0, far_count), :, mine_half], fw_s))
    arrive((head(part_in, far_count), rs_s))
    arrive((part_in, tw_s))

    @pl.when(me.row == 0)
    def _():
        arrive((block.at[pl.ds(0, far_count), :, pl.ds(0, RANK)], mark_s))


def on_device(points, weights, targets, block_index):
    features, owned = points.shape
    count = weights.shape[0]
    rows = lax.axis_size("row_0") * lax.axis_size("row_1")
    cols = lax.axis_size("col_0") * lax.axis_size("col_1")
    group = block_index.shape[1] // rows
    width = group // cols
    depth = features + TAIL
    piece = RANK // rows // lax.axis_size("col_1")
    wide = RANK + 128

    def arrays(kind, *shapes):
        return [pltpu.VMEM(shape, kind) for shape in shapes]

    cores = lax.axis_size("col_1")
    chips = cols // cores
    half = group // cores
    each = count // cols
    scratch = [
        *arrays(BF16, (features, owned)),
        *arrays(F32, (count, owned), (count, owned)),
        *arrays(jnp.int32, (1, group)),
        *arrays(BF16, (cols, features, width)),
        *arrays(F32, (cols, count, width)),
        *arrays(BF16, (cols, features, width)),
        *arrays(F32, (cols, count, width)),
        *arrays(BF16, (depth, width), (rows, depth, group), (depth, RANK)),
        *arrays(BF16, (owned, depth), (rows * width, depth), (count, owned)),
        *arrays(F32, (RANK, group)),
        *arrays(F32, (rows, cores, piece, RANK), (rows, piece, RANK), (piece, RANK)),
        *arrays(F32, (cores, rows, piece, RANK), (RANK, RANK), (RANK, RANK), (32, 128)),
        *arrays(F32, *[(rows, count, half)] * 5),
        *arrays(F32, (chips, count, width), (chips, count, width)),
        *arrays(BF16, (rows * width, group)),
        *arrays(F32, (RANK, half)),
        *arrays(F32, (2, cols, each, wide), (2, cols, each, wide), (2, each, wide)),
        *arrays(F32, (2, rows, each, wide), (2, each, wide), (2, cols, each, wide)),
        *arrays(F32, (count, 128), (rows, count, 128)),
        *arrays(F32, (count, 128), (cols, count, 128)),
        *arrays(F32, (2, count, width), (2, rows, count, width)),
        *arrays(F32, (2, count, group), (2, count, group)),
        *arrays(F32, (2, cols, count, width), (2, cols, count, width)),
        *arrays(F32, (2, count, owned)),
        *arrays(BF16, (depth, rows * width), (3 * RANK, rows * width)),
        *arrays(BF16, (3, RANK, 2 * group)),
    ]
    dma = pltpu.SemaphoreType.DMA
    scratch += [dma((21,)), dma((21,)), dma((4,)), dma, dma]
    scratch += [dma, dma((rows,)), dma, dma((rows,)), dma, dma, dma, dma((rows,))]
    return tuple(
        pl.pallas_call(
            step_kernel,
            out_shape=[
                jax.ShapeDtypeStruct((count, owned), F32),
                jax.ShapeDtypeStruct((count, width), F32),
            ],
            in_specs=[pl.BlockSpec(memory_space=pl.ANY)] * 4,
            scratch_shapes=scratch,
            compiler_params=pltpu.CompilerParams(
                vmem_limit_bytes=60 * 2**20, collective_id=0, has_side_effects=True
            ),
            name="step",
        )(points, weights, targets, block_index)
    )


def solution(mesh):
    split = Mesh(mesh.devices.reshape(4, 4, 4, 2), AXES)
    spec = P(None, AXES)
    return jax.shard_map(
        on_device,
        mesh=split,
        in_specs=(spec, spec, spec, P()),
        out_specs=(spec, spec),
        check_vma=False,
    )
```

```python
import math

import jax
import jax.numpy as jnp
from jax import lax
from jax.experimental import pallas as pl
from jax.experimental.pallas import tpu as pltpu
from jax.sharding import Mesh
from jax.sharding import PartitionSpec as P

RANK = 256
ridge = 1.0
AXES = ("row_0", "row_1", "col_0", "col_1")
MESH = pl.DeviceIdType.MESH
HI = lax.Precision.HIGHEST
F32 = jnp.float32
BF16 = jnp.bfloat16
LOG2E = math.log2(math.e)
TAIL = 16


def wrap(value, size):
    return lax.rem(value, size)


class Place:
    def __init__(self):
        self.sizes = tuple(lax.axis_size(a) for a in AXES)
        self.at = tuple(lax.axis_index(a) for a in AXES)
        ny, nz, nx, nc = self.sizes
        self.rows, self.cols = ny * nz, nx * nc
        self.row = self.at[0] * nz + self.at[1]
        self.col = self.at[2] * nc + self.at[3]
        self.device = self.row * self.cols + self.col

        def hops(step, size):
            return min(step, size - step)

        self.row_steps = sorted(
            ((a, b) for a in range(ny) for b in range(nz) if a or b),
            key=lambda s: -(hops(s[0], ny) + hops(s[1], nz)),
        )
        self.col_steps = sorted(
            ((a, b) for a in range(nx) for b in range(nc) if a or b),
            key=lambda s: -(2 * hops(s[0], nx) + s[1]),
        )

    def row_peer(self, step):
        y = wrap(self.at[0] + step[0], self.sizes[0])
        z = wrap(self.at[1] + step[1], self.sizes[1])
        return y * self.sizes[1] + z, (y, z, self.at[2], self.at[3])

    def col_peer(self, step):
        x = wrap(self.at[2] + step[0], self.sizes[2])
        c = wrap(self.at[3] + step[1], self.sizes[3])
        return x * self.sizes[3] + c, (self.at[0], self.at[1], x, c)

    def x_peers(self):
        out = []
        for step in range(1, self.sizes[2]):
            x = wrap(self.at[2] + step, self.sizes[2])
            out.append((x, (self.at[0], self.at[1], x, self.at[3])))
        return out

    def twin(self):
        return self.col_peer((0, 1))[1]

    def row_peers(self):
        return [self.row_peer(s) for s in self.row_steps]

    def col_peers(self):
        return [self.col_peer(s) for s in self.col_steps]

    def row_before(self, k):
        ny, nz = self.sizes[:2]
        steps = sorted(
            ((a, b) for a in range(ny) for b in range(nz) if a or b),
            key=lambda s: (min(s[0], ny - s[0]) + min(s[1], nz - s[1]), s),
        )
        ys = sum(a << (2 * i) for i, (a, _) in enumerate(steps))
        zs = sum(b << (2 * i) for i, (_, b) in enumerate(steps))
        ys, zs = (lax.rem(jnp.right_shift(jnp.int32(v), 2 * (k - 1)), 4) for v in (ys, zs))
        behind = (wrap(self.at[0] + ny - ys, ny), wrap(self.at[1] + nz - zs, nz))
        ahead = (wrap(self.at[0] + ys, ny), wrap(self.at[1] + zs, nz))
        return behind[0] * nz + behind[1], behind + self.at[2:], ahead + self.at[2:]

    def greet(self):
        barrier = pltpu.get_barrier_semaphore()
        for _, peer in self.row_peers() + self.col_peers():
            pl.semaphore_signal(barrier, inc=1, device_id=peer, device_id_type=MESH)

    def enter(self):
        pl.semaphore_wait(pltpu.get_barrier_semaphore(), self.rows + self.cols - 2)


class Links:
    def __init__(self, sends, recvs):
        self.sends, self.recvs, self.wholes = sends, recvs, []

    def start(self, peers, source, target, whole):
        at = len(self.wholes)
        self.wholes.append(whole)
        for index, peer in peers:
            pltpu.make_async_remote_copy(
                src_ref=source(index),
                dst_ref=target,
                send_sem=self.sends.at[at],
                recv_sem=self.recvs.at[at],
                device_id=peer,
                device_id_type=MESH,
            ).start()
        return whole, self.recvs.at[at]

    def drain(self):
        for at, whole in enumerate(self.wholes):
            arrive((whole, self.sends.at[at]))


def arrive(exchange):
    whole, semaphore = exchange
    pltpu.make_async_copy(whole, whole, semaphore).wait()


def head(ref, length):
    return ref.at[pl.ds(0, length)]


def lanes(index, width):
    return pl.ds(pl.multiple_of(index * width, width), width)


def thirds(value):
    high = value.astype(BF16).astype(F32)
    rest = value - high
    middle = rest.astype(BF16).astype(F32)
    return high, middle, (rest - middle).astype(BF16).astype(F32)


def tail_rows(values, first):
    squares = -0.5 * jnp.sum(values * values, axis=0, keepdims=True)
    parts = thirds(squares)
    shape = (TAIL, values.shape[1])
    at = lax.broadcasted_iota(jnp.int32, shape, 0)
    ones = 8 - first
    rows = jnp.where((at >= ones) & (at < ones + 3), 1.0, 0.0)
    for i in range(3):
        rows = jnp.where(at == first + i, jnp.broadcast_to(parts[i], shape), rows)
    return rows


def as_left(block):
    values = block.astype(F32)
    body = values.shape[0] - TAIL
    left = jnp.concatenate([values[:body], values[body + 8 :], values[body : body + 8]], axis=0)
    return left.T


def kernel_of(left, right, scale):
    return jnp.exp2(scale * jnp.dot(left, right, preferred_element_type=F32))


def total(ref):
    value = ref[0].astype(F32)
    for i in range(1, ref.shape[0]):
        value = value + ref[i].astype(F32)
    return value


def inverse_8(rows, lane):
    shape = (8, 128)
    sub = lax.broadcasted_iota(jnp.int32, shape, 0)
    cols = [jnp.broadcast_to(rows[:, lane + j : lane + j + 1], shape) for j in range(8)]
    for k in range(8):
        pivot = 1.0 / jnp.broadcast_to(cols[k][k : k + 1, :], shape)
        here = sub == k
        column = cols[k]
        for j in range(8):
            if j != k:
                factor = jnp.broadcast_to(cols[j][k : k + 1, :], shape) * pivot
                cols[j] = jnp.where(here, factor, cols[j] - column * factor)
        cols[k] = jnp.where(here, pivot, -column * pivot)
    return cols


def sweep_8(rows, b):
    shape = (8, 128)
    rows = list(rows)
    lane = lax.broadcasted_iota(jnp.int32, shape, 1)
    sub = lax.broadcasted_iota(jnp.int32, shape, 0)
    cols = inverse_8(rows[b], 8 * b)
    inside = (lane >= 8 * b) & (lane < 8 * b + 8)
    right = jnp.where(inside, (lane - 8 * b == sub).astype(F32), rows[b])
    new = None
    for j in range(8):
        term = cols[j] * jnp.broadcast_to(right[j : j + 1, :], shape)
        new = term if new is None else new + term
    spread = [jnp.broadcast_to(new[j : j + 1, :], shape) for j in range(8)]
    for i in range(4):
        if i != b:
            acc = None
            for j in range(8):
                at = 8 * b + j
                term = jnp.broadcast_to(rows[i][:, at : at + 1], shape) * spread[j]
                acc = term if acc is None else acc + term
            rows[i] = jnp.where(inside, 0.0, rows[i]) - acc
    rows[b] = new
    return rows


class Sweep:
    def __init__(self, matrix, k, keep):
        self.matrix, self.keep, self.at = matrix, keep, pl.multiple_of(k * 32, 32)

    def inner(self, b):
        if b == 0:
            size = self.matrix.shape[0]
            rows = self.matrix[pl.ds(self.at, 32), :]
            block = pltpu.roll(rows, lax.rem(size - self.at, size), 1)[:, :128]
            self.small = [block[8 * i : 8 * i + 8, :] for i in range(4)]
        self.small = sweep_8(self.small, b)
        if b == 3:
            self.keep[...] = jnp.concatenate(self.small, axis=0)

    def finish(self):
        matrix, at, size = self.matrix, self.at, self.matrix.shape[0]
        rows = matrix[pl.ds(at, 32), :]
        lane = lax.broadcasted_iota(jnp.int32, (32, size), 1)
        sub = lax.broadcasted_iota(jnp.int32, (32, size), 0)
        wide = lax.broadcasted_iota(jnp.int32, (size, size), 1)
        inv = self.keep[:, :32]
        inside = (lane >= at) & (lane < at + 32)
        right = jnp.where(inside, (lane - at == sub).astype(F32), rows)
        new = jnp.dot(inv, right, precision=HI, preferred_element_type=F32)
        left = jnp.where(lane < at, -rows, rows)
        update = lax.dot_general(
            left, new, (((0,), (0,)), ((), ())), precision=HI, preferred_element_type=F32
        )
        matrix[...] = jnp.where((wide >= at) & (wide < at + 32), 0.0, matrix[...]) - update
        matrix[pl.ds(at, 32), :] = new


def end_kernel(weights, change, residual, weights_out, residual_out):
    weights_out[...] = weights[...] + change[...]
    residual_out[...] = residual[...]


def step_kernel(points_in, weights_in, targets_in, index_in, change, residual, *scratch):
    (
        points, weights, targets, index,
        piece, vpiece, pin, vin, share, block, marks,
        own_left, col_left, weights_bf, sketch,
        gram_part, gram_in, gram_own, gram_all, inner, inverse, keep,
        part_mine, part_other, part_twin, part_sum, part_in, cut_part, cut_in, tile,
        half_sketch, proj_own, proj_in, proj_sum, proj_row, proj_all, proj_out,
        dots_own, dots_row, dots_sum, dots_col,
        vec_own, vec_all, vec_col, dir_col, im_part, im_in, moved,
        col_right, col_sketch, pair,
        sends, recvs, loads, mark_s, mark_r, ag_s, ag_r, fw_s, fw_r, rs_s, rs_r, tw_s, tw_r,
    ) = scratch
    me = Place()
    rows, _, group = block.shape
    here = index_in.at[:, lanes(me.row, group)]
    pairs = [(points_in, points), (here, index), (targets_in, targets), (weights_in, weights)]
    taken = [pltpu.make_async_copy(a, b, loads.at[i]) for i, (a, b) in enumerate(pairs)]
    for copy in taken:
        copy.start()
    me.greet()
    links = Links(sends, recvs)
    near_count, far_count = me.cols - 1, rows - 1
    for copy in taken:
        copy.wait()
    features, owned = points.shape
    count = weights.shape[0]
    width = group // me.cols
    half = group // 2
    span = min(512, owned)
    scale = 4.0 / features * LOG2E
    pieces = [slice(c * span, (c + 1) * span) for c in range(owned // span)]
    my_lanes = lanes(me.col, width)

    local = index[...] - me.device * owned
    own = targets[...] - ridge * weights[...]
    own = [p.astype(BF16) for p in thirds(own)]
    acc = None
    for c, cut in enumerate(pieces):
        at = lax.broadcasted_iota(jnp.int32, (span, group), 0) + c * span
        chosen = jnp.where(at == local, 1.0, 0.0).astype(BF16)
        left = jnp.concatenate([points[:, cut]] + [p[:, cut] for p in own], axis=0)
        some = jnp.dot(left, chosen, preferred_element_type=F32)
        acc = some if acc is None else acc + some
    for c in range(me.cols):
        cut = slice(c * width, (c + 1) * width)
        piece[c] = acc[:features, cut].astype(BF16)
        parts = acc[features:, cut]
        vpiece[c] = parts[:count] + (parts[count : 2 * count] + parts[2 * count :])
    me.enter()
    first = links.start(
        me.col_peers(), lambda c: piece.at[c], pin.at[me.col], head(pin, near_count)
    )
    pin[me.col] = piece[me.col]
    vin[me.col] = vpiece[me.col]
    for cut in pieces:
        some = points[:, cut].astype(F32)
        left = jnp.concatenate([some, tail_rows(some, 8)], axis=0)
        own_left[cut, :] = left.T.astype(BF16)
    weights_bf[...] = weights[...].astype(BF16)
    arrive(first)
    mine = total(pin)
    mine = jnp.concatenate([mine, tail_rows(mine, 0)], axis=0).astype(BF16)
    share[...] = mine
    block[me.row, :, my_lanes] = mine
    most = block.at[me.row, :, pl.ds(0, near_count * width)]
    first = links.start(me.col_peers(), lambda c: share, block.at[me.row, :, my_lanes], most)
    second = links.start(
        me.col_peers(), lambda c: vpiece.at[c], vin.at[me.col], head(vin, near_count)
    )
    arrive(first)

    def mark_copy(i):
        return pltpu.make_async_remote_copy(
            src_ref=block.at[0, :, pl.ds(0, RANK)],
            dst_ref=marks,
            send_sem=mark_s,
            recv_sem=mark_r,
            device_id=me.row_peers()[i][1],
            device_id_type=MESH,
        )

    @pl.when(me.row == 0)
    def _():
        for i in range(rows - 1):
            mark_copy(i).start()
        marks[...] = block[0, :, :RANK]

    mine_half = pl.ds(pl.multiple_of(me.at[3] * half, half), half)

    def ahead_copy(k):
        _, _, peer = me.row_before(k)
        return pltpu.make_async_remote_copy(
            src_ref=block.at[me.row, :, mine_half],
            dst_ref=block.at[me.row, :, mine_half],
            send_sem=ag_s,
            recv_sem=ag_r.at[k],
            device_id=peer,
            device_id_type=MESH,
        )

    def twin_copy(k):
        row, _, _ = me.row_before(k)
        return pltpu.make_async_remote_copy(
            src_ref=block.at[row, :, mine_half],
            dst_ref=block.at[row, :, mine_half],
            send_sem=fw_s,
            recv_sem=fw_r.at[k],
            device_id=me.twin(),
            device_id_type=MESH,
        )

    def half_copy(k):
        return pltpu.make_async_remote_copy(
            src_ref=part_other.at[k],
            dst_ref=part_twin.at[k],
            send_sem=tw_s,
            recv_sem=tw_r.at[k],
            device_id=me.twin(),
            device_id_type=MESH,
        )

    def sum_copy(k):
        _, peer, _ = me.row_before(k)
        return pltpu.make_async_remote_copy(
            src_ref=part_sum.at[k],
            dst_ref=part_in.at[me.row],
            send_sem=rs_s,
            recv_sem=rs_r,
            device_id=peer,
            device_id_type=MESH,
        )

    def ahead_start(k, carry):
        ahead_copy(k).start()
        return carry

    deep = 5
    lax.fori_loop(1, deep, ahead_start, 0)

    def beside(piece, sweep, last):
        if piece == 0 and last is not None:
            last.finish()
        if piece > 0 and sweep is not None:
            sweep.inner(piece - 1)

    def slab(row, sweep=None, last=None):
        right = block[row]
        out = None
        for c, cut in enumerate(pieces):
            beside(c, sweep, last)
            kern = kernel_of(own_left[cut, :], right, scale).astype(BF16)
            some = jnp.dot(weights_bf[:, cut], kern, preferred_element_type=F32)
            out = some if out is None else out + some
        beside(len(pieces), sweep, last)
        mine = block[row, :, my_lanes]
        col_right[:, lanes(row, width)] = mine
        left = as_left(mine)
        col_left[pl.ds(pl.multiple_of(row * width, width), width), :] = left.astype(BF16)
        return out

    def pass_on(k):
        ahead_copy(k).wait_recv()
        twin_copy(k).start()

    def of_core(value, core):
        odd = [value[:, c * width : (c + 1) * width] for c in range(1, me.cols, 2)]
        even = [value[:, c * width : (c + 1) * width] for c in range(0, me.cols, 2)]
        return jnp.where(core == 0, jnp.concatenate(even, axis=1), jnp.concatenate(odd, axis=1))

    def slab_start(k, row, sweep=None, last=None):
        value = slab(row, sweep, last)
        part_mine[k] = of_core(value, me.at[3])
        part_other[k] = of_core(value, 1 - me.at[3])
        half_copy(k).start()

    def settle(k):
        half_copy(k).wait_recv()
        part_sum[k] = part_mine[k] + part_twin[k]
        sum_copy(k).start()

    def slab_step(k, carry, settles=True, sweeps=None, ends=False):
        pl.when(k + deep - 1 < rows)(lambda: ahead_copy(k + deep - 1).start())
        pl.when(k + 1 < rows)(lambda: pass_on(k + 1))
        twin_copy(k).wait_recv()
        sweep = None if sweeps is None else Sweep(inverse, k - sweeps, keep)
        last = Sweep(inverse, k - sweeps - 1, keep) if ends else None
        slab_start(k, me.row_before(k)[0], sweep, last)
        if settles:
            settle(k - 1)
        return carry

    slab_start(0, me.row)

    pass_on(1)
    slab_step(1, 0, settles=False)
    half_copy(0).wait_recv()
    part_in[me.row] = part_mine[0] + part_twin[0]

    @pl.when(me.row != 0)
    def _():
        mark_copy(0).wait_recv()

    marks_left = as_left(marks[...]).astype(BF16)
    sketch[...] = kernel_of(marks_left, block[me.row], scale)
    turned = (((1,), (1,)), ((), ()))
    sk = sketch[...]
    gram = lax.dot_general(sk, sk, turned, precision=HI, preferred_element_type=F32)
    gram_part[...] = gram.reshape(gram_part.shape)
    gram_in[me.row] = gram_part[me.row, me.at[3]]
    third = links.start(
        me.row_peers(),
        lambda r: gram_part.at[r, me.at[3]],
        gram_in.at[me.row],
        head(gram_in, far_count),
    )
    half_sketch[...] = of_core(sk, me.at[3])
    lax.fori_loop(2, 5, slab_step, 0)
    arrive(third)
    mine = total(gram_in)
    gram_own[...] = mine
    gram_all[me.at[3], me.row] = mine
    its_half = gram_all.at[me.at[3]]
    third = links.start(
        me.row_peers(), lambda r: gram_own, its_half.at[me.row], head(its_half, far_count)
    )
    lax.fori_loop(5, 8, slab_step, 0)
    arrive(third)
    third = links.start([(0, me.twin())], lambda r: its_half, its_half, its_half)
    lax.fori_loop(8, 9, slab_step, 0)
    landmarks = kernel_of(marks_left, marks[...], scale)
    arrive(third)
    gram = jnp.concatenate([gram_all[0], gram_all[1]], axis=1).reshape(inner.shape)
    inner[...] = ridge * landmarks + gram
    inverse[...] = inner[...]
    slab_step(9, 0, sweeps=9)
    lax.fori_loop(10, rows, lambda k, carry: slab_step(k, carry, sweeps=9, ends=True), 0)

    right = block[me.row]
    sweep, last = Sweep(inverse, rows - 9, keep), Sweep(inverse, rows - 10, keep)
    parts = rows * width // span
    for c in range(parts):
        cut = slice(c * span, (c + 1) * span)
        beside(c, sweep, last)
        tile[cut, :] = kernel_of(col_left[cut, :], right, scale).astype(BF16)
        if c == 1:
            settle(rows - 1)
    beside(parts, sweep, last)

    parts = thirds(kernel_of(marks_left, col_right[...], scale))
    for i, some in enumerate(parts):
        col_sketch[i * RANK : (i + 1) * RANK, :] = some.astype(BF16)
    quarter = group // 4

    def pair_piece(c):
        cut = slice(c * quarter, (c + 1) * quarter)
        got = jnp.dot(col_sketch[...], tile[:, cut], preferred_element_type=F32)
        got = got[:RANK] + (got[RANK : 2 * RANK] + got[2 * RANK :])
        for i, some in enumerate(thirds(got)):
            pair[i, :, cut] = some.astype(BF16)

    pair_piece(0)
    pair_piece(1)
    arrive(second)

    arrive((head(part_in, far_count), rs_r))
    summed = -total(part_in)
    cuts = [slice(c * width, (c + 1) * width) for c in range(me.cols)]

    def at_share(value, place, places):
        at = lax.broadcasted_iota(jnp.int32, (count, places * width), 1) // width
        return jnp.where(at == place, jnp.concatenate([value] * places, axis=1), 0.0)

    def of_share(value):
        at = lax.broadcasted_iota(jnp.int32, (count, group), 1) // width
        return jnp.where(at == me.col, value, 0.0)

    chips = me.sizes[2]
    summed = summed + at_share(total(vin), me.at[2], chips)
    for c in range(chips):
        cut_part[c] = summed[:, c * width : (c + 1) * width]
    cut_in[me.at[2]] = cut_part[me.at[2]]
    each = count // me.cols

    def sum_start(turn, value):
        for c in range(me.cols):
            proj_own[turn, c] = value[c * each : (c + 1) * each]
        proj_in[turn, me.col] = proj_own[turn, me.col]
        return links.start(
            me.col_peers(),
            lambda c: proj_own.at[turn, c],
            proj_in.at[turn, me.col],
            head(proj_in.at[turn], near_count),
        )

    def sum_rows(turn, copies):
        arrive(copies)
        mine = total(proj_in.at[turn])
        proj_sum[turn] = mine
        proj_row[turn, me.row] = mine
        landing, whole = proj_row.at[turn, me.row], head(proj_row.at[turn], far_count)
        return links.start(me.row_peers(), lambda r: proj_sum.at[turn], landing, whole)

    def sum_back(turn, copies):
        arrive(copies)
        mine = total(proj_row.at[turn])
        proj_all[turn] = mine
        proj_out[turn, me.col] = mine
        landing, whole = proj_out.at[turn, me.col], head(proj_out.at[turn], near_count)
        return links.start(me.col_peers(), lambda c: proj_all.at[turn], landing, whole)

    def sum_end(turn, copies):
        arrive(copies)
        return jnp.concatenate([proj_out[turn, c] for c in range(me.cols)], axis=0)

    def project(vector, marks_of):
        return lax.dot_general(
            vector, marks_of[...], turned, precision=HI, preferred_element_type=F32
        )

    def project_pair(vector):
        parts = [p.astype(BF16) for p in thirds(vector)]
        out = []
        for i in range(3):
            left = jnp.concatenate(parts[: 3 - i], axis=0)
            right = pair[i, :, group:]
            got = lax.dot_general(left, right, turned, preferred_element_type=F32)
            out.append([got[j * count : (j + 1) * count] for j in range(3 - i)])
        return out[0][0] + ((out[0][1] + out[1][0]) + (out[0][2] + (out[1][1] + out[2][0])))

    def solve(projected):
        def product(left, right):
            return jnp.dot(left, right[...], precision=HI, preferred_element_type=F32)

        solved = product(projected, inverse)
        return solved + product(projected - product(solved, inner), inverse)

    def times_pair(vector):
        parts = [p.astype(BF16) for p in thirds(vector)]
        out = []
        for i in range(3):
            left = jnp.concatenate(parts[: 3 - i], axis=0)
            got = jnp.dot(left, pair[i], preferred_element_type=F32)
            out.append([got[j * count : (j + 1) * count] for j in range(3 - i)])
        got = out[0][0] + ((out[0][1] + out[1][0]) + (out[0][2] + (out[1][1] + out[2][0])))
        return got[:, :group], got[:, group:]

    def spread(turn, value):
        vec_own[turn] = value
        vec_all[turn, me.row] = value
        landing, whole = vec_all.at[turn, me.row], head(vec_all.at[turn], far_count)
        far = links.start(me.row_peers(), lambda r: vec_own.at[turn], landing, whole)
        vec_col[turn, :, my_lanes] = value
        landing = vec_col.at[turn, :, my_lanes]
        whole = vec_col.at[turn, :, pl.ds(0, near_count * width)]
        return far, links.start(me.col_peers(), lambda c: vec_own.at[turn], landing, whole)

    def block_times(turn):
        value = jnp.concatenate([vec_all[turn, r] for r in range(rows)], axis=1)
        value = jnp.concatenate([p.astype(BF16) for p in thirds(value)], axis=0)
        got = jnp.dot(value, tile[...], preferred_element_type=F32)
        return got[:count] + (got[count : 2 * count] + got[2 * count :])

    def image_start(turn, value):
        for c, cut in enumerate(cuts):
            im_part[turn, c] = value[:, cut]
        im_in[turn, me.col] = im_part[turn, me.col]
        return links.start(
            me.col_peers(),
            lambda c: im_part.at[turn, c],
            im_in.at[turn, me.col],
            head(im_in.at[turn], near_count),
        )

    def image_end(turn, copies):
        arrive(copies)
        return total(im_in.at[turn])

    lane = lax.broadcasted_iota(jnp.int32, (count, 128), 1)

    def dots(*pairs):
        out = jnp.zeros((count, 128), F32)
        for i, (a, b) in enumerate(pairs):
            out = jnp.where(lane == i, jnp.sum(a * b, axis=1, keepdims=True), out)
        return out

    pad = jnp.zeros((count, 128), F32)
    going = sum_start(0, jnp.concatenate([project(summed, half_sketch), pad], axis=1))
    near = links.start(
        me.x_peers(), lambda c: cut_part.at[c], cut_in.at[me.at[2]], head(cut_in, chips - 1)
    )
    sweep.finish()
    pair_piece(2)
    pair_piece(3)
    for i, some in enumerate(thirds(sketch[...])):
        pair[i, :, group:] = some.astype(BF16)
    going = sum_rows(0, going)
    arrive(near)
    res = total(cut_in)
    far, near = spread(0, res)
    going = sum_back(0, going)
    arrive(far)
    block_res = block_times(0)
    arrive(near)
    res_row = vec_col[0]
    projected = sum_end(0, going)[:, :RANK]
    image_part, back = times_pair(solve(projected))
    direction = (res_row - back) / ridge
    dir_col[0] = direction
    image_part = (block_res - image_part) / ridge + of_share(ridge * direction)
    scalars = dots((direction, image_part), (of_share(direction), res_row))
    going = sum_start(1, jnp.concatenate([project_pair(image_part), scalars], axis=1))
    near = image_start(0, image_part)
    going = sum_rows(1, going)
    image = image_end(0, near)
    far, near = spread(1, image)
    going = sum_back(1, going)
    arrive(far)
    block_image = block_times(1)
    arrive(near)
    image_row = vec_col[1]
    packed = sum_end(1, going)
    curve, old_rz = packed[:, RANK : RANK + 1], packed[:, RANK + 1 : RANK + 2]
    alpha = old_rz / curve
    res = res - alpha * image
    res_row = res_row - alpha * image_row
    image_part, back = times_pair(solve(projected - alpha * packed[:, :RANK]))
    precond = (res_row - back) / ridge
    dir_col[1] = precond
    image_part = (block_res - alpha * block_image - image_part) / ridge
    image_part = image_part + of_share(ridge * precond)
    mine = of_share(precond)
    scalars = dots(
        (precond, image_part), (direction, image_part), (mine, image_row), (mine, res_row)
    )
    dots_own[...] = scalars
    dots_row[me.row] = scalars
    going = links.start(
        me.row_peers(), lambda r: dots_own, dots_row.at[me.row], head(dots_row, far_count)
    )
    near = image_start(1, image_part)
    both = [p.astype(BF16) for turn in range(2) for p in thirds(dir_col[turn])]
    both = jnp.concatenate(both, axis=0)
    for c, cut in enumerate(pieces):
        at = lax.broadcasted_iota(jnp.int32, (span, group), 0) + c * span
        chosen = jnp.where(at == local, 1.0, 0.0).astype(BF16)
        got = lax.dot_general(both, chosen, turned, preferred_element_type=F32)
        for turn in range(2):
            base = 3 * count * turn
            low = got[base + count : base + 2 * count] + got[base + 2 * count : base + 3 * count]
            moved[turn, :, cut] = got[base : base + count] + low
    image_2 = image_end(1, near)
    arrive(going)
    middle = total(dots_row)
    dots_sum[...] = middle
    dots_col[me.col] = middle
    arrive(
        links.start(
            me.col_peers(), lambda c: dots_sum, dots_col.at[me.col], head(dots_col, near_count)
        )
    )
    summed = total(dots_col)
    own_curve, cross_b, cross_a, fresh = (summed[:, i : i + 1] for i in range(4))
    beta = fresh / old_rz
    last_curve = own_curve + beta * (cross_a + cross_b) + beta * beta * curve
    step = fresh / last_curve
    residual[...] = res - step * (image_2 + beta * image)
    change[...] = (alpha + step * beta) * moved[0] + step * moved[1]
    links.drain()
    arrive((block.at[pl.ds(0, far_count), :, mine_half], ag_s))
    arrive((block.at[pl.ds(0, far_count), :, mine_half], fw_s))
    arrive((head(part_in, far_count), rs_s))
    arrive((part_in, tw_s))

    @pl.when(me.row == 0)
    def _():
        arrive((block.at[pl.ds(0, far_count), :, pl.ds(0, RANK)], mark_s))


def on_device(points, weights, targets, block_index):
    features, owned = points.shape
    count = weights.shape[0]
    rows = lax.axis_size("row_0") * lax.axis_size("row_1")
    cols = lax.axis_size("col_0") * lax.axis_size("col_1")
    group = block_index.shape[1] // rows
    width = group // cols
    depth = features + TAIL
    piece = RANK // rows // lax.axis_size("col_1")
    wide = RANK + 128

    def arrays(kind, *shapes):
        return [pltpu.VMEM(shape, kind) for shape in shapes]

    cores = lax.axis_size("col_1")
    chips = cols // cores
    half = group // cores
    each = count // cols
    scratch = [
        *arrays(BF16, (features, owned)),
        *arrays(F32, (count, owned), (count, owned)),
        *arrays(jnp.int32, (1, group)),
        *arrays(BF16, (cols, features, width)),
        *arrays(F32, (cols, count, width)),
        *arrays(BF16, (cols, features, width)),
        *arrays(F32, (cols, count, width)),
        *arrays(BF16, (depth, width), (rows, depth, group), (depth, RANK)),
        *arrays(BF16, (owned, depth), (rows * width, depth), (count, owned)),
        *arrays(F32, (RANK, group)),
        *arrays(F32, (rows, cores, piece, RANK), (rows, piece, RANK), (piece, RANK)),
        *arrays(F32, (cores, rows, piece, RANK), (RANK, RANK), (RANK, RANK), (32, 128)),
        *arrays(F32, *[(rows, count, half)] * 5),
        *arrays(F32, (chips, count, width), (chips, count, width)),
        *arrays(BF16, (rows * width, group)),
        *arrays(F32, (RANK, half)),
        *arrays(F32, (2, cols, each, wide), (2, cols, each, wide), (2, each, wide)),
        *arrays(F32, (2, rows, each, wide), (2, each, wide), (2, cols, each, wide)),
        *arrays(F32, (count, 128), (rows, count, 128)),
        *arrays(F32, (count, 128), (cols, count, 128)),
        *arrays(F32, (2, count, width), (2, rows, count, width)),
        *arrays(F32, (2, count, group), (2, count, group)),
        *arrays(F32, (2, cols, count, width), (2, cols, count, width)),
        *arrays(F32, (2, count, owned)),
        *arrays(BF16, (depth, rows * width), (3 * RANK, rows * width)),
        *arrays(BF16, (3, RANK, 2 * group)),
    ]
    dma = pltpu.SemaphoreType.DMA
    scratch += [dma((21,)), dma((21,)), dma((4,)), dma, dma]
    scratch += [dma, dma((rows,)), dma, dma((rows,)), dma, dma, dma, dma((rows,))]
    outs = [
        jax.ShapeDtypeStruct((count, owned), F32),
        jax.ShapeDtypeStruct((count, width), F32),
    ]
    change, residual = pl.pallas_call(
        step_kernel,
        out_shape=outs,
        in_specs=[pl.BlockSpec(memory_space=pl.ANY)] * 4,
        scratch_shapes=scratch,
        compiler_params=pltpu.CompilerParams(
            vmem_limit_bytes=60 * 2**20, collective_id=0, has_side_effects=True
        ),
        name="step",
    )(points, weights, targets, block_index)
    return tuple(
        pl.pallas_call(end_kernel, out_shape=outs, name="end")(weights, change, residual)
    )


def solution(mesh):
    split = Mesh(mesh.devices.reshape(4, 4, 4, 2), AXES)
    spec = P(None, AXES)
    return jax.shard_map(
        on_device,
        mesh=split,
        in_specs=(spec, spec, spec, P()),
        out_specs=(spec, spec),
        check_vma=False,
    )
```

```python
import math

import jax
import jax.numpy as jnp
from jax import lax
from jax.experimental import pallas as pl
from jax.experimental.pallas import tpu as pltpu
from jax.sharding import Mesh
from jax.sharding import PartitionSpec as P

RANK = 256
ridge = 1.0
AXES = ("row_0", "row_1", "col_0", "col_1")
MESH = pl.DeviceIdType.MESH
HI = lax.Precision.HIGHEST
F32 = jnp.float32
BF16 = jnp.bfloat16
LOG2E = math.log2(math.e)
TAIL = 16


def wrap(value, size):
    return lax.rem(value, size)


class Place:
    def __init__(self):
        self.sizes = tuple(lax.axis_size(a) for a in AXES)
        self.at = tuple(lax.axis_index(a) for a in AXES)
        ny, nz, nx, nc = self.sizes
        self.rows, self.cols = ny * nz, nx * nc
        self.row = self.at[0] * nz + self.at[1]
        self.col = self.at[2] * nc + self.at[3]
        self.device = self.row * self.cols + self.col

        def hops(step, size):
            return min(step, size - step)

        self.row_steps = sorted(
            ((a, b) for a in range(ny) for b in range(nz) if a or b),
            key=lambda s: -(hops(s[0], ny) + hops(s[1], nz)),
        )
        self.col_steps = sorted(
            ((a, b) for a in range(nx) for b in range(nc) if a or b),
            key=lambda s: -(2 * hops(s[0], nx) + s[1]),
        )

    def row_peer(self, step):
        y = wrap(self.at[0] + step[0], self.sizes[0])
        z = wrap(self.at[1] + step[1], self.sizes[1])
        return y * self.sizes[1] + z, (y, z, self.at[2], self.at[3])

    def col_peer(self, step):
        x = wrap(self.at[2] + step[0], self.sizes[2])
        c = wrap(self.at[3] + step[1], self.sizes[3])
        return x * self.sizes[3] + c, (self.at[0], self.at[1], x, c)

    def x_peers(self):
        out = []
        for step in range(1, self.sizes[2]):
            x = wrap(self.at[2] + step, self.sizes[2])
            out.append((x, (self.at[0], self.at[1], x, self.at[3])))
        return out

    def twin(self):
        return self.col_peer((0, 1))[1]

    def row_peers(self):
        return [self.row_peer(s) for s in self.row_steps]

    def col_peers(self):
        return [self.col_peer(s) for s in self.col_steps]

    def row_before(self, k):
        ny, nz = self.sizes[:2]
        steps = sorted(
            ((a, b) for a in range(ny) for b in range(nz) if a or b),
            key=lambda s: (min(s[0], ny - s[0]) + min(s[1], nz - s[1]), s),
        )
        ys = sum(a << (2 * i) for i, (a, _) in enumerate(steps))
        zs = sum(b << (2 * i) for i, (_, b) in enumerate(steps))
        ys, zs = (lax.rem(jnp.right_shift(jnp.int32(v), 2 * (k - 1)), 4) for v in (ys, zs))
        behind = (wrap(self.at[0] + ny - ys, ny), wrap(self.at[1] + nz - zs, nz))
        ahead = (wrap(self.at[0] + ys, ny), wrap(self.at[1] + zs, nz))
        return behind[0] * nz + behind[1], behind + self.at[2:], ahead + self.at[2:]

    def greet(self):
        barrier = pltpu.get_barrier_semaphore()
        for _, peer in self.row_peers() + self.col_peers():
            pl.semaphore_signal(barrier, inc=1, device_id=peer, device_id_type=MESH)

    def enter(self):
        pl.semaphore_wait(pltpu.get_barrier_semaphore(), self.rows + self.cols - 2)


class Links:
    def __init__(self, sends, recvs):
        self.sends, self.recvs, self.wholes = sends, recvs, []

    def start(self, peers, source, target, whole):
        at = len(self.wholes)
        self.wholes.append(whole)
        for index, peer in peers:
            pltpu.make_async_remote_copy(
                src_ref=source(index),
                dst_ref=target,
                send_sem=self.sends.at[at],
                recv_sem=self.recvs.at[at],
                device_id=peer,
                device_id_type=MESH,
            ).start()
        return whole, self.recvs.at[at]

    def drain(self):
        for at, whole in enumerate(self.wholes):
            arrive((whole, self.sends.at[at]))


def arrive(exchange):
    whole, semaphore = exchange
    pltpu.make_async_copy(whole, whole, semaphore).wait()


def head(ref, length):
    return ref.at[pl.ds(0, length)]


def lanes(index, width):
    return pl.ds(pl.multiple_of(index * width, width), width)


def thirds(value):
    high = value.astype(BF16).astype(F32)
    rest = value - high
    middle = rest.astype(BF16).astype(F32)
    return high, middle, (rest - middle).astype(BF16).astype(F32)


def tail_rows(values, first):
    squares = -0.5 * jnp.sum(values * values, axis=0, keepdims=True)
    parts = thirds(squares)
    shape = (TAIL, values.shape[1])
    at = lax.broadcasted_iota(jnp.int32, shape, 0)
    ones = 8 - first
    rows = jnp.where((at >= ones) & (at < ones + 3), 1.0, 0.0)
    for i in range(3):
        rows = jnp.where(at == first + i, jnp.broadcast_to(parts[i], shape), rows)
    return rows


def as_left(block):
    values = block.astype(F32)
    body = values.shape[0] - TAIL
    left = jnp.concatenate([values[:body], values[body + 8 :], values[body : body + 8]], axis=0)
    return left.T


def kernel_of(left, right, scale):
    return jnp.exp2(scale * jnp.dot(left, right, preferred_element_type=F32))


def total(ref):
    value = ref[0].astype(F32)
    for i in range(1, ref.shape[0]):
        value = value + ref[i].astype(F32)
    return value


def inverse_8(rows, lane):
    shape = (8, 128)
    sub = lax.broadcasted_iota(jnp.int32, shape, 0)
    cols = [jnp.broadcast_to(rows[:, lane + j : lane + j + 1], shape) for j in range(8)]
    for k in range(8):
        pivot = 1.0 / jnp.broadcast_to(cols[k][k : k + 1, :], shape)
        here = sub == k
        column = cols[k]
        for j in range(8):
            if j != k:
                factor = jnp.broadcast_to(cols[j][k : k + 1, :], shape) * pivot
                cols[j] = jnp.where(here, factor, cols[j] - column * factor)
        cols[k] = jnp.where(here, pivot, -column * pivot)
    return cols


def sweep_8(rows, b):
    shape = (8, 128)
    rows = list(rows)
    lane = lax.broadcasted_iota(jnp.int32, shape, 1)
    sub = lax.broadcasted_iota(jnp.int32, shape, 0)
    cols = inverse_8(rows[b], 8 * b)
    inside = (lane >= 8 * b) & (lane < 8 * b + 8)
    right = jnp.where(inside, (lane - 8 * b == sub).astype(F32), rows[b])
    new = None
    for j in range(8):
        term = cols[j] * jnp.broadcast_to(right[j : j + 1, :], shape)
        new = term if new is None else new + term
    spread = [jnp.broadcast_to(new[j : j + 1, :], shape) for j in range(8)]
    for i in range(4):
        if i != b:
            acc = None
            for j in range(8):
                at = 8 * b + j
                term = jnp.broadcast_to(rows[i][:, at : at + 1], shape) * spread[j]
                acc = term if acc is None else acc + term
            rows[i] = jnp.where(inside, 0.0, rows[i]) - acc
    rows[b] = new
    return rows


class Sweep:
    def __init__(self, matrix, k, keep):
        self.matrix, self.keep, self.at = matrix, keep, pl.multiple_of(k * 32, 32)

    def inner(self, b):
        if b == 0:
            size = self.matrix.shape[0]
            rows = self.matrix[pl.ds(self.at, 32), :]
            block = pltpu.roll(rows, lax.rem(size - self.at, size), 1)[:, :128]
            self.small = [block[8 * i : 8 * i + 8, :] for i in range(4)]
        self.small = sweep_8(self.small, b)
        if b == 3:
            self.keep[...] = jnp.concatenate(self.small, axis=0)

    def finish(self):
        matrix, at, size = self.matrix, self.at, self.matrix.shape[0]
        rows = matrix[pl.ds(at, 32), :]
        lane = lax.broadcasted_iota(jnp.int32, (32, size), 1)
        sub = lax.broadcasted_iota(jnp.int32, (32, size), 0)
        wide = lax.broadcasted_iota(jnp.int32, (size, size), 1)
        inv = self.keep[:, :32]
        inside = (lane >= at) & (lane < at + 32)
        right = jnp.where(inside, (lane - at == sub).astype(F32), rows)
        new = jnp.dot(inv, right, precision=HI, preferred_element_type=F32)
        left = jnp.where(lane < at, -rows, rows)
        update = lax.dot_general(
            left, new, (((0,), (0,)), ((), ())), precision=HI, preferred_element_type=F32
        )
        matrix[...] = jnp.where((wide >= at) & (wide < at + 32), 0.0, matrix[...]) - update
        matrix[pl.ds(at, 32), :] = new


def end_kernel(weights, change, residual, weights_out, residual_out):
    weights_out[...] = weights[...] + change[...]
    residual_out[...] = residual[...]


def step_kernel(points_in, weights_in, targets_in, index_in, change, residual, *scratch):
    (
        points, weights, targets, index,
        piece, vpiece, pin, vin, share, block, marks,
        own_left, col_left, weights_bf, sketch,
        gram_part, gram_in, gram_own, gram_all, inner, inverse, keep,
        part_mine, part_other, part_twin, part_sum, part_in, cut_part, cut_in, tile,
        half_sketch, proj_own, proj_in, proj_sum, proj_row, proj_all, proj_out,
        dots_own, dots_row, dots_sum, dots_col,
        vec_own, vec_all, vec_col, dir_col, im_part, im_in, moved,
        col_right, col_sketch, pair,
        sends, recvs, loads, mark_s, mark_r, ag_s, ag_r, fw_s, fw_r, rs_s, rs_r, tw_s, tw_r,
    ) = scratch
    me = Place()
    rows, _, group = block.shape
    here = index_in.at[:, lanes(me.row, group)]
    pairs = [(points_in, points), (here, index), (targets_in, targets), (weights_in, weights)]
    taken = [pltpu.make_async_copy(a, b, loads.at[i]) for i, (a, b) in enumerate(pairs)]
    for copy in taken:
        copy.start()
    me.greet()
    links = Links(sends, recvs)
    near_count, far_count = me.cols - 1, rows - 1
    for copy in taken:
        copy.wait()
    features, owned = points.shape
    count = weights.shape[0]
    width = group // me.cols
    half = group // 2
    span = min(512, owned)
    scale = 4.0 / features * LOG2E
    pieces = [slice(c * span, (c + 1) * span) for c in range(owned // span)]
    my_lanes = lanes(me.col, width)

    local = index[...] - me.device * owned
    own = targets[...] - ridge * weights[...]
    own = [p.astype(BF16) for p in thirds(own)]
    acc = None
    for c, cut in enumerate(pieces):
        at = lax.broadcasted_iota(jnp.int32, (span, group), 0) + c * span
        chosen = jnp.where(at == local, 1.0, 0.0).astype(BF16)
        left = jnp.concatenate([points[:, cut]] + [p[:, cut] for p in own], axis=0)
        some = jnp.dot(left, chosen, preferred_element_type=F32)
        acc = some if acc is None else acc + some
    for c in range(me.cols):
        cut = slice(c * width, (c + 1) * width)
        piece[c] = acc[:features, cut].astype(BF16)
        parts = acc[features:, cut]
        vpiece[c] = parts[:count] + (parts[count : 2 * count] + parts[2 * count :])
    me.enter()
    first = links.start(
        me.col_peers(), lambda c: piece.at[c], pin.at[me.col], head(pin, near_count)
    )
    pin[me.col] = piece[me.col]
    vin[me.col] = vpiece[me.col]
    for cut in pieces:
        some = points[:, cut].astype(F32)
        left = jnp.concatenate([some, tail_rows(some, 8)], axis=0)
        own_left[cut, :] = left.T.astype(BF16)
    weights_bf[...] = weights[...].astype(BF16)
    arrive(first)
    mine = total(pin)
    mine = jnp.concatenate([mine, tail_rows(mine, 0)], axis=0).astype(BF16)
    share[...] = mine
    block[me.row, :, my_lanes] = mine
    most = block.at[me.row, :, pl.ds(0, near_count * width)]
    first = links.start(me.col_peers(), lambda c: share, block.at[me.row, :, my_lanes], most)
    second = links.start(
        me.col_peers(), lambda c: vpiece.at[c], vin.at[me.col], head(vin, near_count)
    )
    arrive(first)

    def mark_copy(i):
        return pltpu.make_async_remote_copy(
            src_ref=block.at[0, :, pl.ds(0, RANK)],
            dst_ref=marks,
            send_sem=mark_s,
            recv_sem=mark_r,
            device_id=me.row_peers()[i][1],
            device_id_type=MESH,
        )

    @pl.when(me.row == 0)
    def _():
        for i in range(rows - 1):
            mark_copy(i).start()
        marks[...] = block[0, :, :RANK]

    mine_half = pl.ds(pl.multiple_of(me.at[3] * half, half), half)

    def ahead_copy(k):
        _, _, peer = me.row_before(k)
        return pltpu.make_async_remote_copy(
            src_ref=block.at[me.row, :, mine_half],
            dst_ref=block.at[me.row, :, mine_half],
            send_sem=ag_s,
            recv_sem=ag_r.at[k],
            device_id=peer,
            device_id_type=MESH,
        )

    def twin_copy(k):
        row, _, _ = me.row_before(k)
        return pltpu.make_async_remote_copy(
            src_ref=block.at[row, :, mine_half],
            dst_ref=block.at[row, :, mine_half],
            send_sem=fw_s,
            recv_sem=fw_r.at[k],
            device_id=me.twin(),
            device_id_type=MESH,
        )

    def half_copy(k):
        return pltpu.make_async_remote_copy(
            src_ref=part_other.at[k],
            dst_ref=part_twin.at[k],
            send_sem=tw_s,
            recv_sem=tw_r.at[k],
            device_id=me.twin(),
            device_id_type=MESH,
        )

    def sum_copy(k):
        _, peer, _ = me.row_before(k)
        return pltpu.make_async_remote_copy(
            src_ref=part_sum.at[k],
            dst_ref=part_in.at[me.row],
            send_sem=rs_s,
            recv_sem=rs_r,
            device_id=peer,
            device_id_type=MESH,
        )

    def ahead_start(k, carry):
        ahead_copy(k).start()
        return carry

    deep = 5
    lax.fori_loop(1, deep, ahead_start, 0)

    def beside(piece, sweep, last):
        if piece == 0 and last is not None:
            last.finish()
        if piece > 0 and sweep is not None:
            sweep.inner(piece - 1)

    def slab(row, sweep=None, last=None):
        right = block[row]
        out = None
        for c, cut in enumerate(pieces):
            beside(c, sweep, last)
            kern = kernel_of(own_left[cut, :], right, scale).astype(BF16)
            some = jnp.dot(weights_bf[:, cut], kern, preferred_element_type=F32)
            out = some if out is None else out + some
        beside(len(pieces), sweep, last)
        mine = block[row, :, my_lanes]
        col_right[:, lanes(row, width)] = mine
        left = as_left(mine)
        col_left[pl.ds(pl.multiple_of(row * width, width), width), :] = left.astype(BF16)
        return out

    def pass_on(k):
        ahead_copy(k).wait_recv()
        twin_copy(k).start()

    def of_core(value, core):
        odd = [value[:, c * width : (c + 1) * width] for c in range(1, me.cols, 2)]
        even = [value[:, c * width : (c + 1) * width] for c in range(0, me.cols, 2)]
        return jnp.where(core == 0, jnp.concatenate(even, axis=1), jnp.concatenate(odd, axis=1))

    def slab_start(k, row, sweep=None, last=None):
        value = slab(row, sweep, last)
        part_mine[k] = of_core(value, me.at[3])
        part_other[k] = of_core(value, 1 - me.at[3])
        half_copy(k).start()

    def settle(k):
        half_copy(k).wait_recv()
        part_sum[k] = part_mine[k] + part_twin[k]
        sum_copy(k).start()

    def slab_step(k, carry, settles=True, sweeps=None, ends=False):
        pl.when(k + deep - 1 < rows)(lambda: ahead_copy(k + deep - 1).start())
        pl.when(k + 1 < rows)(lambda: pass_on(k + 1))
        twin_copy(k).wait_recv()
        sweep = None if sweeps is None else Sweep(inverse, k - sweeps, keep)
        last = Sweep(inverse, k - sweeps - 1, keep) if ends else None
        slab_start(k, me.row_before(k)[0], sweep, last)
        if settles:
            settle(k - 1)
        return carry

    slab_start(0, me.row)

    pass_on(1)
    slab_step(1, 0, settles=False)
    half_copy(0).wait_recv()
    part_in[me.row] = part_mine[0] + part_twin[0]

    @pl.when(me.row != 0)
    def _():
        mark_copy(0).wait_recv()

    marks_left = as_left(marks[...]).astype(BF16)
    sketch[...] = kernel_of(marks_left, block[me.row], scale)
    turned = (((1,), (1,)), ((), ()))
    sk = sketch[...]
    gram = lax.dot_general(sk, sk, turned, precision=HI, preferred_element_type=F32)
    gram_part[...] = gram.reshape(gram_part.shape)
    gram_in[me.row] = gram_part[me.row, me.at[3]]
    third = links.start(
        me.row_peers(),
        lambda r: gram_part.at[r, me.at[3]],
        gram_in.at[me.row],
        head(gram_in, far_count),
    )
    half_sketch[...] = of_core(sk, me.at[3])
    lax.fori_loop(2, 5, slab_step, 0)
    arrive(third)
    mine = total(gram_in)
    gram_own[...] = mine
    gram_all[me.at[3], me.row] = mine
    its_half = gram_all.at[me.at[3]]
    third = links.start(
        me.row_peers(), lambda r: gram_own, its_half.at[me.row], head(its_half, far_count)
    )
    lax.fori_loop(5, 8, slab_step, 0)
    arrive(third)
    third = links.start([(0, me.twin())], lambda r: its_half, its_half, its_half)
    lax.fori_loop(8, 9, slab_step, 0)
    landmarks = kernel_of(marks_left, marks[...], scale)
    arrive(third)
    gram = jnp.concatenate([gram_all[0], gram_all[1]], axis=1).reshape(inner.shape)
    inner[...] = ridge * landmarks + gram
    inverse[...] = inner[...]
    slab_step(9, 0, sweeps=9)
    lax.fori_loop(10, rows, lambda k, carry: slab_step(k, carry, sweeps=9, ends=True), 0)

    right = block[me.row]
    sweep, last = Sweep(inverse, rows - 9, keep), Sweep(inverse, rows - 10, keep)
    parts = rows * width // span
    for c in range(parts):
        cut = slice(c * span, (c + 1) * span)
        beside(c, sweep, last)
        tile[cut, :] = kernel_of(col_left[cut, :], right, scale).astype(BF16)
        if c == 1:
            settle(rows - 1)
    beside(parts, sweep, last)

    parts = thirds(kernel_of(marks_left, col_right[...], scale))
    for i, some in enumerate(parts):
        col_sketch[i * RANK : (i + 1) * RANK, :] = some.astype(BF16)
    quarter = group // 4

    def pair_piece(c):
        cut = slice(c * quarter, (c + 1) * quarter)
        got = jnp.dot(col_sketch[...], tile[:, cut], preferred_element_type=F32)
        got = got[:RANK] + (got[RANK : 2 * RANK] + got[2 * RANK :])
        for i, some in enumerate(thirds(got)):
            pair[i, :, cut] = some.astype(BF16)

    pair_piece(0)
    pair_piece(1)
    arrive(second)

    arrive((head(part_in, far_count), rs_r))
    summed = -total(part_in)
    cuts = [slice(c * width, (c + 1) * width) for c in range(me.cols)]

    def at_share(value, place, places):
        at = lax.broadcasted_iota(jnp.int32, (count, places * width), 1) // width
        return jnp.where(at == place, jnp.concatenate([value] * places, axis=1), 0.0)

    def of_share(value):
        at = lax.broadcasted_iota(jnp.int32, (count, group), 1) // width
        return jnp.where(at == me.col, value, 0.0)

    chips = me.sizes[2]
    summed = summed + at_share(total(vin), me.at[2], chips)
    for c in range(chips):
        cut_part[c] = summed[:, c * width : (c + 1) * width]
    cut_in[me.at[2]] = cut_part[me.at[2]]
    each = count // me.cols

    def sum_start(turn, value):
        for c in range(me.cols):
            proj_own[turn, c] = value[c * each : (c + 1) * each]
        proj_in[turn, me.col] = proj_own[turn, me.col]
        return links.start(
            me.col_peers(),
            lambda c: proj_own.at[turn, c],
            proj_in.at[turn, me.col],
            head(proj_in.at[turn], near_count),
        )

    def sum_rows(turn, copies):
        arrive(copies)
        mine = total(proj_in.at[turn])
        proj_sum[turn] = mine
        proj_row[turn, me.row] = mine
        landing, whole = proj_row.at[turn, me.row], head(proj_row.at[turn], far_count)
        return links.start(me.row_peers(), lambda r: proj_sum.at[turn], landing, whole)

    def sum_back(turn, copies):
        arrive(copies)
        mine = total(proj_row.at[turn])
        proj_all[turn] = mine
        proj_out[turn, me.col] = mine
        landing, whole = proj_out.at[turn, me.col], head(proj_out.at[turn], near_count)
        return links.start(me.col_peers(), lambda c: proj_all.at[turn], landing, whole)

    def sum_end(turn, copies):
        arrive(copies)
        return jnp.concatenate([proj_out[turn, c] for c in range(me.cols)], axis=0)

    def project(vector, marks_of):
        return lax.dot_general(
            vector, marks_of[...], turned, precision=HI, preferred_element_type=F32
        )

    def project_pair(vector):
        parts = [p.astype(BF16) for p in thirds(vector)]
        out = []
        for i in range(3):
            left = jnp.concatenate(parts[: 3 - i], axis=0)
            right = pair[i, :, group:]
            got = lax.dot_general(left, right, turned, preferred_element_type=F32)
            out.append([got[j * count : (j + 1) * count] for j in range(3 - i)])
        return out[0][0] + ((out[0][1] + out[1][0]) + (out[0][2] + (out[1][1] + out[2][0])))

    def solve(projected):
        def product(left, right):
            return jnp.dot(left, right[...], precision=HI, preferred_element_type=F32)

        solved = product(projected, inverse)
        return solved + product(projected - product(solved, inner), inverse)

    def times_pair(vector):
        parts = [p.astype(BF16) for p in thirds(vector)]
        out = []
        for i in range(3):
            left = jnp.concatenate(parts[: 3 - i], axis=0)
            got = jnp.dot(left, pair[i], preferred_element_type=F32)
            out.append([got[j * count : (j + 1) * count] for j in range(3 - i)])
        got = out[0][0] + ((out[0][1] + out[1][0]) + (out[0][2] + (out[1][1] + out[2][0])))
        return got[:, :group], got[:, group:]

    def spread(turn, value):
        vec_own[turn] = value
        vec_all[turn, me.row] = value
        landing, whole = vec_all.at[turn, me.row], head(vec_all.at[turn], far_count)
        far = links.start(me.row_peers(), lambda r: vec_own.at[turn], landing, whole)
        vec_col[turn, :, my_lanes] = value
        landing = vec_col.at[turn, :, my_lanes]
        whole = vec_col.at[turn, :, pl.ds(0, near_count * width)]
        return far, links.start(me.col_peers(), lambda c: vec_own.at[turn], landing, whole)

    def block_times(turn):
        value = jnp.concatenate([vec_all[turn, r] for r in range(rows)], axis=1)
        value = jnp.concatenate([p.astype(BF16) for p in thirds(value)], axis=0)
        got = jnp.dot(value, tile[...], preferred_element_type=F32)
        return got[:count] + (got[count : 2 * count] + got[2 * count :])

    def image_start(turn, value):
        for c, cut in enumerate(cuts):
            im_part[turn, c] = value[:, cut]
        im_in[turn, me.col] = im_part[turn, me.col]
        return links.start(
            me.col_peers(),
            lambda c: im_part.at[turn, c],
            im_in.at[turn, me.col],
            head(im_in.at[turn], near_count),
        )

    def image_end(turn, copies):
        arrive(copies)
        return total(im_in.at[turn])

    lane = lax.broadcasted_iota(jnp.int32, (count, 128), 1)

    def dots(*pairs):
        out = jnp.zeros((count, 128), F32)
        for i, (a, b) in enumerate(pairs):
            out = jnp.where(lane == i, jnp.sum(a * b, axis=1, keepdims=True), out)
        return out

    pad = jnp.zeros((count, 128), F32)
    going = sum_start(0, jnp.concatenate([project(summed, half_sketch), pad], axis=1))
    near = links.start(
        me.x_peers(), lambda c: cut_part.at[c], cut_in.at[me.at[2]], head(cut_in, chips - 1)
    )
    sweep.finish()
    pair_piece(2)
    pair_piece(3)
    for i, some in enumerate(thirds(sketch[...])):
        pair[i, :, group:] = some.astype(BF16)
    going = sum_rows(0, going)
    arrive(near)
    res = total(cut_in)
    far, near = spread(0, res)
    going = sum_back(0, going)
    arrive(far)
    block_res = block_times(0)
    arrive(near)
    res_row = vec_col[0]
    projected = sum_end(0, going)[:, :RANK]
    image_part, back = times_pair(solve(projected))
    direction = (res_row - back) / ridge
    dir_col[0] = direction
    image_part = (block_res - image_part) / ridge + of_share(ridge * direction)
    scalars = dots((direction, image_part), (of_share(direction), res_row))
    going = sum_start(1, jnp.concatenate([project_pair(image_part), scalars], axis=1))
    near = image_start(0, image_part)
    going = sum_rows(1, going)
    image = image_end(0, near)
    far, near = spread(1, image)
    going = sum_back(1, going)
    arrive(far)
    block_image = block_times(1)
    arrive(near)
    image_row = vec_col[1]
    packed = sum_end(1, going)
    curve, old_rz = packed[:, RANK : RANK + 1], packed[:, RANK + 1 : RANK + 2]
    alpha = old_rz / curve
    res = res - alpha * image
    res_row = res_row - alpha * image_row
    image_part, back = times_pair(solve(projected - alpha * packed[:, :RANK]))
    precond = (res_row - back) / ridge
    dir_col[1] = precond
    image_part = (block_res - alpha * block_image - image_part) / ridge
    image_part = image_part + of_share(ridge * precond)
    mine = of_share(precond)
    scalars = dots(
        (precond, image_part), (direction, image_part), (mine, image_row), (mine, res_row)
    )
    scalars = jnp.concatenate([scalars.T[:8], jnp.zeros((8, 128 - count), F32)], axis=1)
    dots_own[...] = scalars
    dots_row[me.row] = scalars
    going = links.start(
        me.row_peers(), lambda r: dots_own, dots_row.at[me.row], head(dots_row, far_count)
    )
    near = image_start(1, image_part)
    both = [p.astype(BF16) for turn in range(2) for p in thirds(dir_col[turn])]
    both = jnp.concatenate(both, axis=0)
    for c, cut in enumerate(pieces):
        at = lax.broadcasted_iota(jnp.int32, (span, group), 0) + c * span
        chosen = jnp.where(at == local, 1.0, 0.0).astype(BF16)
        got = lax.dot_general(both, chosen, turned, preferred_element_type=F32)
        for turn in range(2):
            base = 3 * count * turn
            low = got[base + count : base + 2 * count] + got[base + 2 * count : base + 3 * count]
            moved[turn, :, cut] = got[base : base + count] + low
    image_2 = image_end(1, near)
    arrive(going)
    middle = total(dots_row)
    dots_sum[...] = middle
    dots_col[me.col] = middle
    arrive(
        links.start(
            me.col_peers(), lambda c: dots_sum, dots_col.at[me.col], head(dots_col, near_count)
        )
    )
    summed = total(dots_col).T[:count]
    own_curve, cross_b, cross_a, fresh = (summed[:, i : i + 1] for i in range(4))
    beta = fresh / old_rz
    last_curve = own_curve + beta * (cross_a + cross_b) + beta * beta * curve
    step = fresh / last_curve
    residual[...] = res - step * (image_2 + beta * image)
    change[...] = (alpha + step * beta) * moved[0] + step * moved[1]
    links.drain()
    arrive((block.at[pl.ds(0, far_count), :, mine_half], ag_s))
    arrive((block.at[pl.ds(0, far_count), :, mine_half], fw_s))
    arrive((head(part_in, far_count), rs_s))
    arrive((part_in, tw_s))

    @pl.when(me.row == 0)
    def _():
        arrive((block.at[pl.ds(0, far_count), :, pl.ds(0, RANK)], mark_s))


def on_device(points, weights, targets, block_index):
    features, owned = points.shape
    count = weights.shape[0]
    rows = lax.axis_size("row_0") * lax.axis_size("row_1")
    cols = lax.axis_size("col_0") * lax.axis_size("col_1")
    group = block_index.shape[1] // rows
    width = group // cols
    depth = features + TAIL
    piece = RANK // rows // lax.axis_size("col_1")
    wide = RANK + 128

    def arrays(kind, *shapes):
        return [pltpu.VMEM(shape, kind) for shape in shapes]

    cores = lax.axis_size("col_1")
    chips = cols // cores
    half = group // cores
    each = count // cols
    scratch = [
        *arrays(BF16, (features, owned)),
        *arrays(F32, (count, owned), (count, owned)),
        *arrays(jnp.int32, (1, group)),
        *arrays(BF16, (cols, features, width)),
        *arrays(F32, (cols, count, width)),
        *arrays(BF16, (cols, features, width)),
        *arrays(F32, (cols, count, width)),
        *arrays(BF16, (depth, width), (rows, depth, group), (depth, RANK)),
        *arrays(BF16, (owned, depth), (rows * width, depth), (count, owned)),
        *arrays(F32, (RANK, group)),
        *arrays(F32, (rows, cores, piece, RANK), (rows, piece, RANK), (piece, RANK)),
        *arrays(F32, (cores, rows, piece, RANK), (RANK, RANK), (RANK, RANK), (32, 128)),
        *arrays(F32, *[(rows, count, half)] * 5),
        *arrays(F32, (chips, count, width), (chips, count, width)),
        *arrays(BF16, (rows * width, group)),
        *arrays(F32, (RANK, half)),
        *arrays(F32, (2, cols, each, wide), (2, cols, each, wide), (2, each, wide)),
        *arrays(F32, (2, rows, each, wide), (2, each, wide), (2, cols, each, wide)),
        *arrays(F32, (8, 128), (rows, 8, 128)),
        *arrays(F32, (8, 128), (cols, 8, 128)),
        *arrays(F32, (2, count, width), (2, rows, count, width)),
        *arrays(F32, (2, count, group), (2, count, group)),
        *arrays(F32, (2, cols, count, width), (2, cols, count, width)),
        *arrays(F32, (2, count, owned)),
        *arrays(BF16, (depth, rows * width), (3 * RANK, rows * width)),
        *arrays(BF16, (3, RANK, 2 * group)),
    ]
    dma = pltpu.SemaphoreType.DMA
    scratch += [dma((21,)), dma((21,)), dma((4,)), dma, dma]
    scratch += [dma, dma((rows,)), dma, dma((rows,)), dma, dma, dma, dma((rows,))]
    outs = [
        jax.ShapeDtypeStruct((count, owned), F32),
        jax.ShapeDtypeStruct((count, width), F32),
    ]
    change, residual = pl.pallas_call(
        step_kernel,
        out_shape=outs,
        in_specs=[pl.BlockSpec(memory_space=pl.ANY)] * 4,
        scratch_shapes=scratch,
        compiler_params=pltpu.CompilerParams(
            vmem_limit_bytes=60 * 2**20, collective_id=0, has_side_effects=True
        ),
        name="step",
    )(points, weights, targets, block_index)
    return tuple(
        pl.pallas_call(end_kernel, out_shape=outs, name="end")(weights, change, residual)
    )


def solution(mesh):
    split = Mesh(mesh.devices.reshape(4, 4, 4, 2), AXES)
    spec = P(None, AXES)
    return jax.shard_map(
        on_device,
        mesh=split,
        in_specs=(spec, spec, spec, P()),
        out_specs=(spec, spec),
        check_vma=False,
    )
```
